256 devices in a mesh: prow: 16 (over y_lo, z), pcol: 16 (over y_hi, x, core).
Axes of the slice: x: 4, y: 4 (y_hi: 2, y_lo: 2; y = y_hi * 2 + y_lo), z: 8, core: 2. Of those that a mesh axis runs over, the one named last changes fastest.
Arguments:
- ainv: float32 [3, 16, 256, 3, 16, 256], P(None, 'prow', None, None, 'pcol')
- panel: float32 [4, 3, 16, 256, 256], P(None, None, 'prow', 'pcol'), may hold values from -6 to 6
- diag_inv: float32 [4, 256, 256], replicated, may hold values from -0.03125 to 0.03125
- dinv: float32 [4, 256, 256], replicated, may hold values from -6 to 6
- present: int32 [4, 48], replicated, may hold values from 0 to 1, as said below
Outputs:
- column_blocks: float32 [4, 3, 16, 256, 256], P(None, None, 'prow', 'pcol')
- diag_blocks: float32 [4, 256, 256], replicated
The draws below stay inside these ranges and needn't reach their ends.
Inputs may be any that keep to these rules, and one draw needn't show every extreme that they name: `present`: each supernode lists between 60 percent (rounded up) and all of the 48 blocks; one supernode lists all of them and one exactly (148) // 5.
All inputs are finite; a program needn't handle non-finite values.
Results may differ from the reference program's by a relative error of at most 0.000071.
Values sent between devices are 32-bit elements; how exact they have to be, the bound alone decides.
No kernel may reach another device: no remote copies, remote signals or barrier semaphores. Data moves between devices by JAX's collectives and lax.ppermute only.
A program may use at most 64 MiB of HBM per device.

```python
import jax
import jax.numpy as jnp
from jax import lax

SN = 4
B = 256
RB = 3
NB = 48
CB = 3
M = 12288
N_PROW = 16
N_PCOL = 16


def draw_ainv(key, part):
    first = jax.random.fold_in(key, 11)
    second = jax.random.fold_in(key, 12)
    noise = jax.random.normal(first, (M, M), jnp.float32) * M ** (-0.5)
    shift = jax.random.uniform(second, (M,), jnp.float32, -0.5, 0.5)
    full = noise + jnp.diag(shift)
    return full.reshape(RB, N_PROW, B, CB, N_PCOL, B)


def draw_present(key, part):
    key_counts = jax.random.fold_in(key, 21)
    key_order = jax.random.fold_in(key, 22)
    key_perm = jax.random.fold_in(key, 23)
    lowest = (3 * NB + 4) // 5
    extra = jax.random.randint(key_counts, (SN - 2,), lowest, NB + 1)
    counts = jnp.concatenate([jnp.array([NB, lowest], jnp.int32), extra.astype(jnp.int32)])
    counts = jax.random.permutation(key_order, counts)
    keys = jax.random.split(key_perm, SN)
    orders = jax.vmap(lambda k: jax.random.permutation(k, NB))(keys)
    ranks = jnp.argsort(orders, axis=1)
    return (ranks < counts[:, None]).astype(jnp.int32)


def block_scale(stream_key, dims, cuts, least, high):
    def one(position, shards_of):
        heights = jax.random.uniform(jax.random.fold_in(jax.random.fold_in(stream_key, 6), position), (shards_of,), jnp.float32, least / len(cuts), high / len(cuts))
        return jnp.repeat(jnp.exp(heights), dims[position] // shards_of).reshape((-1,) + (1,) * (len(dims) - position - 1))

    loudness = one(*cuts[0])
    for cut in cuts[1:]:
        loudness = loudness * one(*cut)
    return loudness


def scatter_about(rng, dims, scale, most, pieces=(), held_as=jnp.bfloat16):
    drawn = jax.random.normal(rng, dims, jnp.float32) * scale
    if len(pieces) > 0:
        drawn = block_scale(rng, dims, pieces, -0.22, 0.18) * drawn
    return jnp.clip(drawn, min=-most, max=most).astype(held_as)


def setup_inputs(seed: int = 0) -> dict:
    arg_keys = jax.random.split(jax.random.key(seed), 6)
    return {
        "ainv": draw_ainv(jax.random.fold_in(arg_keys[5], 71), 0),
        "panel": scatter_about(arg_keys[1], (SN, RB, N_PROW, B, B), 1.0, 6.0, ((2, 16), (3, 16)), jnp.float32),
        "diag_inv": scatter_about(arg_keys[2], (SN, B, B), (B * 128) ** -0.5, 0.03125, (), jnp.float32),
        "dinv": scatter_about(arg_keys[3], (SN, B, B), 1.0, 6.0, (), jnp.float32),
        "present": draw_present(jax.random.fold_in(arg_keys[5], 71), 0),
    }


def reference(ainv, panel, diag_inv, dinv, present):
    matrix = ainv.reshape(M, M)
    panels = panel.reshape(SN, M, B)
    row_mask = jnp.repeat(present.astype(jnp.float32), B, axis=1)
    lhat = jnp.einsum("smc,scd->smd", panels, diag_inv, precision=lax.Precision.HIGHEST) * row_mask[:, :, None]

    def one(slab):
        return -jnp.dot(matrix, slab, precision=lax.Precision.HIGHEST, preferred_element_type=jnp.float32)

    blocks = lax.map(one, lhat)
    diag_blocks = dinv - jnp.einsum("smc,smd->scd", lhat, blocks, precision=lax.Precision.HIGHEST)
    return blocks.reshape(SN, RB, N_PROW, B, B), diag_blocks
```

```python
import functools

import jax
import jax.numpy as jnp
from jax import lax
from jax.experimental import pallas as pl
from jax.experimental.pallas import tpu as pltpu
from jax.sharding import PartitionSpec as P

F32 = jnp.float32
BF16 = jnp.bfloat16
CHUNKS = ((0, 2), (2, 4))
HIGHEST = lax.Precision.HIGHEST

BOTH = ("prow", "pcol")
SMEM = pl.BlockSpec(memory_space=pltpu.SMEM)
VMEM = pl.BlockSpec(memory_space=pltpu.VMEM)


def swap_grid(v):
    return lax.ppermute(v, BOTH, [(p * 16 + q, q * 16 + p) for p in range(16) for q in range(16)])


def flip_prow(v, mask):
    return lax.ppermute(v, "prow", [(p, p ^ mask) for p in range(16)])


def shift_z(v, d):
    return lax.ppermute(v, "prow", [(p, (p // 8) * 8 + (p + d) % 8) for p in range(16)])


def swap_core(v):
    return lax.ppermute(v, "pcol", [(q, q ^ 1) for q in range(16)])


def shift_plane(v, dx, dyh):
    def to(q):
        return ((q // 8 + dyh) % 2) * 8 + ((q // 2 + dx) % 4) * 2 + q % 2

    return lax.ppermute(v, "pcol", [(q, to(q)) for q in range(16)])


def shift_y(v, d):
    pairs = []
    for p in range(16):
        for q in range(16):
            y = ((q // 8) * 2 + p // 8 + d) % 4
            pairs.append((p * 16 + q, ((y % 2) * 8 + p % 8) * 16 + (y // 2) * 8 + q % 8))
    return lax.ppermute(v, BOTH, pairs)


def call(body, outs, specs, scratch=(), flops=0):
    return pl.pallas_call(
        body,
        out_shape=outs,
        in_specs=specs,
        out_specs=jax.tree.map(lambda _: VMEM, outs),
        scratch_shapes=list(scratch),
        compiler_params=pltpu.CompilerParams(vmem_limit_bytes=48 << 20),
        cost_estimate=pl.CostEstimate(flops=flops, transcendentals=0, bytes_accessed=4 << 20),
    )


def split_two(v):
    high = v.astype(BF16)
    return high, (v - high.astype(F32)).astype(BF16)


def matrix_body(rows, a, high, low):
    @pl.loop(0, 16)
    def _(g):
        start = pl.multiple_of(rows[g] * 16, 16)
        for i in range(3):
            h, l = split_two(-a[i, pl.ds(start, 16), :])
            at = pl.multiple_of(g * 48 + i * 16, 16)
            high[pl.ds(at, 16), :] = h
            low[pl.ds(at, 16), :] = l


def product_body(tab, high, low, *refs):
    pieces, (keep, send, lh, ll) = refs[:-4], refs[-4:]
    z, yl = tab[0], tab[1]
    count = keep.shape[1]

    def put(block, s, flip, d):
        start = pl.multiple_of(((yl + flip) % 2) * 128 + ((z - d + 8) % 8) * 16, 16)
        h, l = split_two(block)
        for i in range(3):
            lh[s, pl.ds(i * 256 + start, 16), :] = h[i * 16 : i * 16 + 16]
            ll[s, pl.ds(i * 256 + start, 16), :] = l[i * 16 : i * 16 + 16]

    dot = functools.partial(jnp.dot, preferred_element_type=F32)

    @pl.loop(0, count)
    def _(s):
        for ref, d in zip(pieces[:7], (0, 1, 2, 3, -1, -2, -3)):
            for flip in range(2):
                put(ref[flip, s], s, flip, d)
        put(pieces[7][s], s, 0, 4)
        put(pieces[8][s], s, 1, 4)
        for half, out in enumerate((keep, send)):
            at = slice(half * 384, half * 384 + 384)
            value = dot(high[at, :], ll[s]) + dot(low[at, :], lh[s]) + dot(high[at, :], lh[s])
            for k in range(8):
                out[k, s] = value[k * 48 : k * 48 + 48]


def halves_body(a, b, *outs):
    for k in range(8):
        outs[k][...] = a[k] + b[k]


def sum_body(*refs):
    refs[-1][...] = sum((r[...] for r in refs[1:-1]), refs[0][...])


def term_body(tab, la, lb, sa, sb, *refs):
    outs, held = refs[:4], refs[4]
    x, core = tab[3], tab[4]
    cols = pl.ds(pl.multiple_of(core * 128, 128), 128)
    for s in range(4):
        for k, (l, r) in enumerate(((la, sa), (lb, sb))):
            value = lax.dot_general(
                l[s, :, cols], r[s], (((0,), (0,)), ((), ())),
                precision=HIGHEST, preferred_element_type=F32,
            )
            held[s] = value if k == 0 else held[s] + value
        for k in range(4):
            outs[k][s] = held[s, pl.ds(pl.multiple_of(((x + k) % 4) * 32, 32), 32), :]


def fold_body(tab, a, b, c, d, *refs):
    outs, held = refs[:4], refs[4]
    y = tab[5]
    held[...] = (a[...] + b[...]) + (c[...] + d[...])
    for k in range(4):
        outs[k][...] = held[:, pl.ds(pl.multiple_of(((y + k) % 4) * 8, 8), 8), :]


def join_body(which, tab, a, b, c, d, out):
    rows = a.shape[1]
    for k, r in enumerate((a, b, c, d)):
        at = pl.multiple_of(((tab[which] - k + 4) % 4) * rows, rows)
        out[:, pl.ds(at, rows), :] = r[...]


def last_body(tab, own, other, dinv, out):
    core = tab[4]
    for k, r in enumerate((own, other)):
        at = pl.ds(pl.multiple_of(((core + k) % 2) * 128, 128), 128)
        out[:, at, :] = dinv[:, at, :] - r[...]


def body(ainv, panel, diag_inv, dinv, present):
    p, q = lax.axis_index("prow"), lax.axis_index("pcol")
    z, yl = p % 8, p // 8
    yh, x, core = q // 8, (q // 2) % 4, q % 2
    tab = jnp.stack([z, yl, yh, x, core, yh * 2 + yl, p, q]).astype(jnp.int32)
    g = jnp.arange(16, dtype=jnp.int32)
    rows = ((yh + g // 4 % 2) % 2) * 8 + ((x + g % 4) % 4) * 2 + (core + g // 8) % 2

    def shape(*dims, dtype=F32):
        return jax.ShapeDtypeStruct(dims, dtype)

    live = lax.dynamic_slice_in_dim(present.reshape(4, 3, 16), p, 1, 2)[:, :, 0]
    lhat = jnp.einsum("sirc,scd->sird", panel[:, :, 0], diag_inv, precision=HIGHEST)
    lhat = (lhat * live.astype(F32)[:, :, None, None]).reshape(4, 48, 256)

    high, low = call(
        matrix_body, [shape(768, 768, dtype=BF16)] * 2, [SMEM, VMEM]
    )(rows, ainv.reshape(3, 256, 768))

    shares = []
    for first, last in CHUNKS:
        n = last - first
        mine = swap_grid(lhat[first:last])
        own = jnp.stack([mine, flip_prow(mine, 8)])
        a1 = shift_z(own, 1)
        b1 = shift_z(own, -1)
        a2 = shift_z(a1, 1)
        b2 = shift_z(b1, -1)
        a3 = shift_z(a2, 1)
        b3 = shift_z(b2, -1)
        a4 = shift_z(a3[0], 1)
        b4 = shift_z(b3[1], -1)
        keep, send = call(
            product_body,
            [shape(8, n, 48, 256)] * 2,
            [SMEM] + [VMEM] * 11,
            [pltpu.VMEM((n, 768, 256), BF16)] * 2,
            flops=6 * 768 * 768 * 256 * n,
        )(tab, high, low, own, a1, a2, a3, b1, b2, b3, a4, b4)
        parts = call(halves_body, [shape(n, 48, 256)] * 8, [VMEM] * 2)(keep, swap_core(send))
        got = [parts[0]] + [shift_plane(parts[k], k % 4, k // 4) for k in range(1, 8)]
        shares.append(call(sum_body, shape(n, 48, 256), [VMEM] * 8)(*got))
    shares = jnp.concatenate(shares, axis=0)

    parts = call(
        term_body, [shape(4, 32, 256)] * 4, [SMEM] + [VMEM] * 4, [pltpu.VMEM((4, 128, 256), F32)]
    )(tab, lhat, swap_core(lhat), shares, swap_core(shares))
    parts = [parts[0]] + [shift_plane(parts[k], k, 0) for k in range(1, 4)]
    parts = call(
        fold_body, [shape(4, 8, 256)] * 4, [SMEM] + [VMEM] * 4, [pltpu.VMEM((4, 32, 256), F32)]
    )(tab, *parts)
    parts = [parts[0]] + [shift_y(parts[k], k) for k in range(1, 4)]
    total = (parts[0] + parts[1]) + (parts[2] + parts[3])
    for mask in (1, 2, 4):
        total = total + flip_prow(total, mask)
    parts = [total] + [shift_y(total, k) for k in range(1, 4)]
    total = call(functools.partial(join_body, 5), shape(4, 32, 256), [SMEM] + [VMEM] * 4)(tab, *parts)
    parts = [total] + [shift_plane(total, k, 0) for k in range(1, 4)]
    total = call(functools.partial(join_body, 3), shape(4, 128, 256), [SMEM] + [VMEM] * 4)(tab, *parts)
    diag = call(last_body, shape(4, 256, 256), [SMEM] + [VMEM] * 3)(
        tab, total, swap_core(total), dinv
    )
    return shares.reshape(4, 3, 1, 16, 256), diag


def solution(mesh):
    return jax.shard_map(
        body,
        mesh=mesh,
        in_specs=(
            P(None, "prow", None, None, "pcol", None),
            P(None, None, "prow", "pcol", None),
            P(),
            P(),
            P(),
        ),
        out_specs=(P(None, None, "prow", "pcol", None), P()),
        check_vma=False,
    )
```

```python
import functools

import jax
import jax.numpy as jnp
from jax import lax
from jax.experimental import pallas as pl
from jax.experimental.pallas import tpu as pltpu
from jax.sharding import Mesh, PartitionSpec as P

F32 = jnp.float32
BF16 = jnp.bfloat16
HIGHEST = lax.Precision.HIGHEST

AXES = ("y_lo", "z", "y_hi", "x", "core")
PLANE = ("y_lo", "y_hi", "x")
LANDING = (0, 4, 1, 6, 2, 7, 3, 5)
SOURCE = tuple(LANDING.index(d) for d in range(8))
SMEM = pl.BlockSpec(memory_space=pltpu.SMEM)
VMEM = pl.BlockSpec(memory_space=pltpu.VMEM)


def to_columns(v):
    pairs = []
    for p in range(16):
        for q in range(16):
            row = (q // 8) * 8 + (p % 8 + LANDING[q % 8]) % 8
            pairs.append((p * 16 + q, row * 16 + p))
    return lax.ppermute(v, AXES, pairs)


def swap_y(v):
    return lax.ppermute(v, "y_lo", [(0, 1), (1, 0)])


def shift_z(v, d):
    return lax.ppermute(v, "z", [(p, (p + d) % 8) for p in range(8)])


def swap_core(v):
    return lax.ppermute(v, "core", [(0, 1), (1, 0)])


def call(body, outs, specs, scratch=(), flops=0, limit=8):
    return pl.pallas_call(
        body,
        out_shape=outs,
        in_specs=specs,
        out_specs=jax.tree.map(lambda _: VMEM, outs),
        scratch_shapes=list(scratch),
        compiler_params=pltpu.CompilerParams(vmem_limit_bytes=limit << 20),
        cost_estimate=pl.CostEstimate(flops=flops, transcendentals=0, bytes_accessed=4 << 20),
    )


def shape(*dims, dtype=F32):
    return jax.ShapeDtypeStruct(dims, dtype)


def split_two(v):
    high = v.astype(BF16)
    return high, (v - high.astype(F32)).astype(BF16)


def panel_body(tab, present, panel, inverse, out):
    p = tab[0]
    for s in range(4):
        value = jnp.dot(panel[s], inverse[s], precision=HIGHEST, preferred_element_type=F32)
        for i in range(3):
            live = present[s, i * 16 + p].astype(F32)
            out[s, i * 16 : i * 16 + 16] = value[i * 16 : i * 16 + 16] * live


def matrix_body(tab, a, high, low):
    core = tab[2]

    @pl.loop(0, 16)
    def _(g):
        start = (g % 8) * 32 + ((core + g // 8) % 2) * 16
        for i in range(3):
            at = pl.multiple_of(g * 48 + i * 16, 16)
            for j in range(3):
                for half in range(2):
                    block = a[pl.ds(((i * 256 + start) * 3 + j) * 2 + half, 16, stride=6), :]
                    h, l = split_two(-block)
                    high[half, pl.ds(at, 16), j * 128 : j * 128 + 128] = h
                    low[half, pl.ds(at, 16), j * 128 : j * 128 + 128] = l


def product_body(flip, tab, high, low, *refs):
    if flip:
        before, pieces = refs[:2], refs[2:11]
    else:
        before, pieces = None, refs[:9]
    outs, (lh, ll) = refs[-4:-2], refs[-2:]
    half = (tab[1] + flip) % 2
    dot = functools.partial(jnp.dot, preferred_element_type=F32)

    def put(block, d):
        start = pl.multiple_of(tab[8 + d % 8], 16)
        h, l = split_two(block)
        for i in range(3):
            lh[pl.ds(i * 128 + start, 16), :] = h[i * 16 : i * 16 + 16]
            ll[pl.ds(i * 128 + start, 16), :] = l[i * 16 : i * 16 + 16]

    @pl.loop(0, 4)
    def _(s):
        for ref, d in zip(pieces[:7], (0, 1, 2, 3, -1, -2, -3)):
            put(ref[s], d)

        @pl.when(s < 2)
        def _():
            put(pieces[7][s % 2], 4)

        @pl.when(s >= 2)
        def _():
            put(pieces[8][s % 2], 4)

        for c in range(2):
            at = slice(c * 384, c * 384 + 384)
            value = (
                dot(high[half, at, :], ll[...])
                + dot(low[half, at, :], lh[...])
                + dot(high[half, at, :], lh[...])
            )
            for k in range(8):
                part = value[k * 48 : k * 48 + 48]
                outs[c][k, s] = part if before is None else before[c][k, s] + part


def term_body(tab, la, lb, sa, sb, out):
    cols = pl.ds(pl.multiple_of(tab[2] * 128, 128), 128)

    @pl.loop(0, 4)
    def _(s):
        value = [
            lax.dot_general(
                l[s, :, cols], r[s], (((0,), (0,)), ((), ())),
                precision=HIGHEST, preferred_element_type=F32,
            )
            for l, r in ((la, sa), (lb, sb))
        ]
        total = value[0] + value[1]
        for e in range(16):
            out[e, s] = total[e * 8 : e * 8 + 8]


def last_body(tab, own, other, dinv, out):
    core = tab[2]
    for k, r in enumerate((own, other)):
        base = pl.multiple_of(((core + k) % 2) * 128, 128)
        for s in range(4):
            for e in range(16):
                at = pl.ds(base + e * 8, 8)
                out[s, at, :] = dinv[s, at, :] - r[e, s]


def body(ainv, panel, diag_inv, dinv, present):
    yl, z, yh, x, core = (lax.axis_index(a) for a in AXES)
    place = jnp.arange(8, dtype=jnp.int32)
    landed = (z - place - (x * 2 + core)) % 8
    source = sum(jnp.where(landed == d, SOURCE[d], 0) for d in range(8))
    head = jnp.stack([yl * 8 + z, yl, core, x, z, yh, yh, yh]).astype(jnp.int32)
    tab = jnp.concatenate([head, (source * 16).astype(jnp.int32)])

    lhat = call(panel_body, shape(4, 48, 256), [SMEM, SMEM, VMEM, VMEM])(
        tab, present, panel.reshape(4, 48, 256), diag_inv
    )
    own = to_columns(lhat)
    mate = swap_core(lhat)
    high, low = call(matrix_body, [shape(2, 768, 384, dtype=BF16)] * 2, [SMEM, VMEM])(
        tab, ainv.reshape(4608, 128)
    )
    own, mate, high, low = lax.optimization_barrier((own, mate, high, low))

    chains = []
    for first in (own, swap_y(own)):
        a1, b1 = shift_z(first, 1), shift_z(first, -1)
        a2, b2 = shift_z(a1, 1), shift_z(b1, -1)
        a3, b3 = shift_z(a2, 1), shift_z(b2, -1)
        a4, b4 = shift_z(a3[:2], 1), shift_z(b3[2:], -1)
        chains.append((first, a1, a2, a3, b1, b2, b3, a4, b4))
    parts = ()
    for flip, pieces in enumerate(chains):
        parts = call(
            functools.partial(product_body, flip),
            [shape(8, 4, 48, 256)] * 2,
            [SMEM] + [VMEM] * (2 + len(parts) + 9),
            [pltpu.VMEM((384, 256), BF16)] * 2,
            flops=6 * 768 * 384 * 1024,
            limit=12,
        )(tab, high, low, *parts, *pieces)
    keep, send = parts
    both = keep + swap_core(send)
    shares = jnp.sum(lax.all_to_all(both, ("y_hi", "x"), 0, 0), axis=0)

    term = call(term_body, shape(16, 4, 8, 256), [SMEM] + [VMEM] * 4)(
        tab, lhat, mate, shares, swap_core(shares)
    )
    total = jnp.sum(lax.all_to_all(term, PLANE, 0, 0), axis=0)
    spread = jnp.broadcast_to(total[None], (8, 4, 8, 256))
    total = jnp.sum(lax.all_to_all(spread, "z", 0, 0), axis=0)
    spread = jnp.broadcast_to(total[None], (16, 4, 8, 256))
    total = lax.all_to_all(spread, PLANE, 0, 0)
    diag = call(last_body, shape(4, 256, 256), [SMEM] + [VMEM] * 3)(
        tab, total, swap_core(total), dinv
    )
    return shares.reshape(4, 3, 1, 16, 256), diag


def solution(mesh):
    fine = Mesh(mesh.devices.reshape(2, 8, 2, 4, 2), AXES)
    rows, columns = ("y_lo", "z"), ("y_hi", "x", "core")
    return jax.shard_map(
        body,
        mesh=fine,
        in_specs=(
            P(None, rows, None, None, columns, None),
            P(None, None, rows, columns, None),
            P(),
            P(),
            P(),
        ),
        out_specs=(P(None, None, rows, columns, None), P()),
        check_vma=False,
    )
```

```python
import functools

import jax
import jax.numpy as jnp
from jax import lax
from jax.experimental import pallas as pl
from jax.experimental.pallas import tpu as pltpu
from jax.sharding import Mesh, PartitionSpec as P


F32 = jnp.float32
BF16 = jnp.bfloat16
HIGHEST = lax.Precision.HIGHEST

AXES = ("y_lo", "z", "y_hi", "x", "core")
PLANE = ("y_lo", "y_hi", "x")
LANDING = (0, 4, 1, 6, 2, 7, 3, 5)
SOURCE = tuple(LANDING.index(d) for d in range(8))
SMEM = pl.BlockSpec(memory_space=pltpu.SMEM)
VMEM = pl.BlockSpec(memory_space=pltpu.VMEM)


def to_columns(v):
    pairs = []
    for p in range(16):
        for q in range(16):
            row = (q // 8) * 8 + (p % 8 + LANDING[q % 8]) % 8
            pairs.append((p * 16 + q, row * 16 + p))
    return lax.ppermute(v, AXES, pairs)


def swap_y(v):
    return lax.ppermute(v, "y_lo", [(0, 1), (1, 0)])


def shift_z(v, d):
    return lax.ppermute(v, "z", [(p, (p + d) % 8) for p in range(8)])


def swap_core(v):
    return lax.ppermute(v, "core", [(0, 1), (1, 0)])


def shift_plane(v, k):
    pairs = []
    for q in range(8):
        pairs.append((q, (q // 4 + k // 4) % 2 * 4 + (q + k) % 4))
    return lax.ppermute(v, ("y_hi", "x"), pairs)


def call(body, outs, specs, scratch=(), flops=0, limit=8):
    return pl.pallas_call(
        body,
        out_shape=outs,
        in_specs=specs,
        out_specs=jax.tree.map(lambda _: VMEM, outs),
        scratch_shapes=list(scratch),
        compiler_params=pltpu.CompilerParams(vmem_limit_bytes=limit << 20),
        cost_estimate=pl.CostEstimate(flops=flops, transcendentals=0, bytes_accessed=4 << 20),
    )


def shape(*dims, dtype=F32):
    return jax.ShapeDtypeStruct(dims, dtype)


def split_two(v):
    high = v.astype(BF16)
    return high, (v - high.astype(F32)).astype(BF16)


def panel_body(which, tab, present, panel, inverse, out):
    p = tab[which]
    for s in range(4):
        value = jnp.dot(panel[s], inverse[s], precision=HIGHEST, preferred_element_type=F32)
        for i in range(3):
            live = present[s, i * 16 + p].astype(F32)
            out[s, i * 16 : i * 16 + 16] = value[i * 16 : i * 16 + 16] * live


def matrix_body(tab, a, out):
    core, x, yh = tab[2], tab[3], tab[5]

    @pl.loop(0, 16)
    def _(g):
        place = (yh + g // 4) % 2 * 4 + (x + g) % 4
        start = place * 32 + ((core + g // 8) % 2) * 16
        for i in range(3):
            at = pl.ds(pl.multiple_of(g * 48 + i * 16, 16), 16)
            for j in range(3):
                for half in range(2):
                    block = a[pl.ds(((i * 256 + start) * 3 + j) * 2 + half, 16, stride=6), :]
                    h, l = split_two(-block)
                    for term, part in enumerate((h, l, h)):
                        col = term * 384 + j * 128
                        out[half, at, col : col + 128] = part


def product_body(flip, sides, tab, matrix, *refs):
    n = len(sides)
    before, pieces = (refs[:n], refs[n : n + 9]) if flip else (None, refs[:9])
    outs, held = refs[-n - 1 : -1], refs[-1]
    half = (tab[1] + flip) % 2

    def put(block, d):
        start = pl.multiple_of(tab[8 + d % 8], 16)
        h, l = split_two(block)
        for i in range(3):
            for term, part in enumerate((l, h, h)):
                held[pl.ds(term * 384 + i * 128 + start, 16), :] = part[i * 16 : i * 16 + 16]

    @pl.loop(0, 4)
    def _(s):
        for ref, d in zip(pieces[:7], (0, 1, 2, 3, -1, -2, -3)):
            put(ref[s], d)

        @pl.when(s < 2)
        def _():
            put(pieces[7][s % 2], 4)

        @pl.when(s >= 2)
        def _():
            put(pieces[8][s % 2], 4)

        for n, c in enumerate(sides):
            value = jnp.dot(
                matrix[half, c * 384 : c * 384 + 384, :], held[...], preferred_element_type=F32
            )
            for k in range(8):
                part = value[k * 48 : k * 48 + 48]
                outs[n][k, s] = part if before is None else before[n][k, s] + part


def halves_body(a, b, *outs):
    for k in range(8):
        outs[k][...] = a[k] + b[k]


def sum_body(*refs):
    value = refs[0][...]
    for r in refs[1:-1]:
        value = value + r[...]
    refs[-1][...] = value


def term_body(tab, la, lb, sa, sb, out):
    cols = pl.ds(pl.multiple_of(tab[2] * 128, 128), 128)

    @pl.loop(0, 4)
    def _(s):
        value = [
            lax.dot_general(
                l[s, :, cols], r[s], (((0,), (0,)), ((), ())),
                precision=HIGHEST, preferred_element_type=F32,
            )
            for l, r in ((la, sa), (lb, sb))
        ]
        total = value[0] + value[1]
        for e in range(16):
            out[e, s] = total[e * 8 : e * 8 + 8]


def last_body(tab, own, other, dinv, out):
    core = tab[2]
    for k, r in enumerate((own, other)):
        base = pl.multiple_of(((core + k) % 2) * 128, 128)
        for s in range(4):
            for e in range(16):
                at = pl.ds(base + e * 8, 8)
                out[s, at, :] = dinv[s, at, :] - r[e, s]


def process(ainv, panel, diag_inv, dinv, present):
    yl, z, yh, x, core = (lax.axis_index(a) for a in AXES)
    place = jnp.arange(8, dtype=jnp.int32)
    landed = (z - place - (x * 2 + core)) % 8
    source = sum(jnp.where(landed == d, SOURCE[d], 0) for d in range(8))
    head = jnp.stack([yl * 8 + z, yl, core, x, z, yh, yh * 8 + x * 2 + core, yh]).astype(jnp.int32)
    tab = jnp.concatenate([head, (source * 16).astype(jnp.int32)])

    panel = panel.reshape(4, 48, 256)

    def normalize(which, rows):
        return call(
            functools.partial(panel_body, which), shape(4, 48, 256), [SMEM, SMEM, VMEM, VMEM]
        )(tab, present, rows, diag_inv)

    arrived = to_columns(panel)
    lhat = normalize(0, panel)
    mate = swap_core(lhat)
    matrix = call(matrix_body, shape(2, 768, 1152, dtype=BF16), [SMEM, VMEM])(
        tab, ainv.reshape(4608, 128)
    )
    arrived, mate, matrix = lax.optimization_barrier((arrived, mate, matrix))
    own = normalize(6, arrived)

    chains = []
    for first in (own, swap_y(own)):
        a1, b1 = shift_z(first, 1), shift_z(first, -1)
        a2, b2 = shift_z(a1, 1), shift_z(b1, -1)
        a3, b3 = shift_z(a2, 1), shift_z(b2, -1)
        a4, b4 = shift_z(a3[:2], 1), shift_z(b3[2:], -1)
        chains.append((first, a1, a2, a3, b1, b2, b3, a4, b4))

    def product(flip, sides, *before):
        return call(
            functools.partial(product_body, flip, sides),
            [shape(8, 4, 48, 256)] * len(sides),
            [SMEM] + [VMEM] * (1 + len(before) + 9),
            [pltpu.VMEM((1152, 256), BF16)],
            flops=3 * 768 * 384 * 1024 * len(sides),
            limit=12,
        )(tab, matrix, *before, *chains[flip])

    keep, send = product(0, (0, 1))
    (send,) = product(1, (1,), send)
    other = swap_core(send)
    (keep,) = product(1, (0,), keep)
    parts = call(halves_body, [shape(4, 48, 256)] * 8, [VMEM] * 2)(keep, other)
    parts = [parts[0]] + [shift_plane(parts[k], k) for k in (6, 5, 7, 4, 2, 1, 3)]
    shares = call(sum_body, shape(4, 48, 256), [VMEM] * 8)(*parts)

    term = call(term_body, shape(16, 4, 8, 256), [SMEM] + [VMEM] * 4)(
        tab, lhat, mate, shares, swap_core(shares)
    )
    total = jnp.sum(lax.all_to_all(term, PLANE, 0, 0), axis=0)
    spread = jnp.broadcast_to(total[None], (8, 4, 8, 256))
    total = jnp.sum(lax.all_to_all(spread, "z", 0, 0), axis=0)
    spread = jnp.broadcast_to(total[None], (16, 4, 8, 256))
    total = lax.all_to_all(spread, PLANE, 0, 0)
    diag = call(last_body, shape(4, 256, 256), [SMEM] + [VMEM] * 3)(
        tab, total, swap_core(total), dinv
    )
    return shares.reshape(4, 3, 1, 16, 256), diag


def solution(mesh):
    fine = Mesh(mesh.devices.reshape(2, 8, 2, 4, 2), AXES)
    rows, columns = ("y_lo", "z"), ("y_hi", "x", "core")
    return jax.shard_map(
        process,
        mesh=fine,
        in_specs=(
            P(None, rows, None, None, columns, None),
            P(None, None, rows, columns, None),
            P(),
            P(),
            P(),
        ),
        out_specs=(P(None, None, rows, columns, None), P()),
        check_vma=False,
    )
```

```python
import functools

import jax
import jax.numpy as jnp
from jax import lax
from jax.experimental import pallas as pl
from jax.experimental.pallas import tpu as pltpu
from jax.sharding import Mesh, PartitionSpec as P


F32 = jnp.float32
BF16 = jnp.bfloat16
HIGHEST = lax.Precision.HIGHEST

AXES = ("y_lo", "z", "y_hi", "x", "core")
PLANE = ("y_lo", "y_hi", "x")
LANDING = (0, 4, 1, 6, 2, 7, 3, 5)
SOURCE = tuple(LANDING.index(d) for d in range(8))
SMEM = pl.BlockSpec(memory_space=pltpu.SMEM)
VMEM = pl.BlockSpec(memory_space=pltpu.VMEM)


def to_columns(v):
    pairs = []
    for p in range(16):
        for q in range(16):
            row = (q // 8) * 8 + (p % 8 + LANDING[q % 8]) % 8
            pairs.append((p * 16 + q, row * 16 + p))
    return lax.ppermute(v, AXES, pairs)


def swap_y(v):
    return lax.ppermute(v, "y_lo", [(0, 1), (1, 0)])


def shift_z(v, d):
    return lax.ppermute(v, "z", [(p, (p + d) % 8) for p in range(8)])


def swap_core(v):
    return lax.ppermute(v, "core", [(0, 1), (1, 0)])


def flip_y(v):
    return lax.ppermute(v, "y_hi", [(0, 1), (1, 0)])


def shift_x(v, d):
    return lax.ppermute(v, "x", [(p, (p + d) % 4) for p in range(4)])


def call(body, outs, specs, scratch=(), flops=0, limit=8):
    return pl.pallas_call(
        body,
        out_shape=outs,
        in_specs=specs,
        out_specs=jax.tree.map(lambda _: VMEM, outs),
        scratch_shapes=list(scratch),
        compiler_params=pltpu.CompilerParams(vmem_limit_bytes=limit << 20),
        cost_estimate=pl.CostEstimate(flops=flops, transcendentals=0, bytes_accessed=4 << 20),
    )


def shape(*dims, dtype=F32):
    return jax.ShapeDtypeStruct(dims, dtype)


def split_two(v):
    high = v.astype(BF16)
    return high, (v - high.astype(F32)).astype(BF16)


def panel_body(which, tab, present, panel, inverse, out):
    p = tab[which]
    for s in range(4):
        value = jnp.dot(panel[s], inverse[s], precision=HIGHEST, preferred_element_type=F32)
        for i in range(3):
            live = present[s, i * 16 + p].astype(F32)
            out[s, i * 16 : i * 16 + 16] = value[i * 16 : i * 16 + 16] * live


def matrix_body(tab, a, out):
    core, x, yh = tab[2], tab[3], tab[5]

    @pl.loop(0, 16)
    def _(g):
        place = (yh + g) % 2 * 4 + (x + g // 2) % 4
        start = place * 32 + ((core + g // 8) % 2) * 16
        for i in range(3):
            at = pl.ds(pl.multiple_of(g * 48 + i * 16, 16), 16)
            for j in range(3):
                for half in range(2):
                    block = a[pl.ds(((i * 256 + start) * 3 + j) * 2 + half, 16, stride=6), :]
                    h, l = split_two(-block)
                    for term, part in enumerate((h, l, h)):
                        col = term * 384 + j * 128
                        out[half, at, col : col + 128] = part


def product_body(flip, sides, tab, matrix, *refs):
    n = len(sides)
    before, pieces = (refs[:n], refs[n : n + 9]) if flip else (None, refs[:9])
    outs, held = refs[-n - 1 : -1], refs[-1]
    half = (tab[1] + flip) % 2

    def put(block, d):
        start = pl.multiple_of(tab[8 + d % 8], 16)
        h, l = split_two(block)
        for i in range(3):
            for term, part in enumerate((l, h, h)):
                held[pl.ds(term * 384 + i * 128 + start, 16), :] = part[i * 16 : i * 16 + 16]

    @pl.loop(0, 4)
    def _(s):
        for ref, d in zip(pieces[:7], (0, 1, 2, 3, -1, -2, -3)):
            put(ref[s], d)

        @pl.when(s < 2)
        def _():
            put(pieces[7][s % 2], 4)

        @pl.when(s >= 2)
        def _():
            put(pieces[8][s % 2], 4)

        for n, c in enumerate(sides):
            value = jnp.dot(
                matrix[half, c * 384 : c * 384 + 384, :], held[...], preferred_element_type=F32
            )
            for k in range(8):
                part = value[k * 48 : k * 48 + 48]
                outs[n][k, s] = part if before is None else before[n][k, s] + part


def spread_body(*refs):
    rows, out, held = refs[:4], refs[4], refs[5]

    @pl.loop(0, 4)
    def _(s):
        for k in range(8):
            held[k * 48 : k * 48 + 48, :] = rows[k // 2][k % 2, s]
        h, l = split_two(held[...].T)
        for term, part in enumerate((h, l, h)):
            out[s, :, term * 384 : term * 384 + 384] = part


def pair_body(tab, keep, other, spread, *refs):
    parts, (mine, yours, held, value) = refs[:4], refs[4:]
    core = tab[2]

    @pl.loop(0, 4)
    def _(s):
        for k in range(8):
            part = keep[k, s] + other[k, s]
            parts[k // 2][k % 2, s] = part
            h, l = split_two(part)
            for term, piece in enumerate((l, h, h)):
                at = term * 384 + k * 48
                held[at : at + 48, :] = piece
        value[...] = jnp.dot(spread[s], held[...], preferred_element_type=F32)
        for out, base in ((mine, core * 128), (yours, 128 - core * 128)):
            for e in range(16):
                out[e, s] = value[pl.ds(pl.multiple_of(base + e * 8, 8), 8), :]


def sum_body(*refs):
    value = refs[0][...]
    for r in refs[1:-1]:
        value = value + r[...]
    refs[-1][...] = value


def last_body(tab, own, other, dinv, out):
    core = tab[2]
    for k, r in enumerate((own, other)):
        base = pl.multiple_of(((core + k) % 2) * 128, 128)
        for s in range(4):
            for e in range(16):
                at = pl.ds(base + e * 8, 8)
                out[s, at, :] = dinv[s, at, :] - r[e, s]


def process(ainv, panel, diag_inv, dinv, present):
    yl, z, yh, x, core = (lax.axis_index(a) for a in AXES)
    place = jnp.arange(8, dtype=jnp.int32)
    landed = (z - place - (x * 2 + core)) % 8
    source = sum(jnp.where(landed == d, SOURCE[d], 0) for d in range(8))
    head = jnp.stack([yl * 8 + z, yl, core, x, z, yh, yh * 8 + x * 2 + core, yh]).astype(jnp.int32)
    tab = jnp.concatenate([head, (source * 16).astype(jnp.int32)])

    panel = panel.reshape(4, 48, 256)

    def normalize(which, rows):
        return call(
            functools.partial(panel_body, which), shape(4, 48, 256), [SMEM, SMEM, VMEM, VMEM]
        )(tab, present, rows, diag_inv)

    arrived = to_columns(panel)
    lhat = normalize(0, panel)
    pair = jnp.stack([lhat, flip_y(lhat)])
    matrix = call(matrix_body, shape(2, 768, 1152, dtype=BF16), [SMEM, VMEM])(
        tab, ainv.reshape(4608, 128)
    )
    arrived, pair, matrix = lax.optimization_barrier((arrived, pair, matrix))
    own = normalize(6, arrived)
    near = [shift_x(pair, -d) for d in (1, 2, 3)]
    spread = call(
        spread_body,
        shape(4, 256, 1152, dtype=BF16),
        [VMEM] * 4,
        [pltpu.VMEM((384, 256), F32)],
    )(pair, *near)

    chains = []
    for first in (own, swap_y(own)):
        a1, b1 = shift_z(first, 1), shift_z(first, -1)
        a2, b2 = shift_z(a1, 1), shift_z(b1, -1)
        a3, b3 = shift_z(a2, 1), shift_z(b2, -1)
        a4, b4 = shift_z(a3[:2], 1), shift_z(b3[2:], -1)
        chains.append((first, a1, a2, a3, b1, b2, b3, a4, b4))

    def product(flip, sides, *before):
        return call(
            functools.partial(product_body, flip, sides),
            [shape(8, 4, 48, 256)] * len(sides),
            [SMEM] + [VMEM] * (1 + len(before) + 9),
            [pltpu.VMEM((1152, 256), BF16)],
            flops=3 * 768 * 384 * 1024 * len(sides),
            limit=12,
        )(tab, matrix, *before, *chains[flip])

    keep, send = product(0, (0, 1))
    keep, send, spread = lax.optimization_barrier((keep, send, spread))
    (send,) = product(1, (1,), send)
    other = swap_core(send)
    (keep,) = product(1, (0,), keep)
    *parts, mine, yours = call(
        pair_body,
        [shape(2, 4, 48, 256)] * 4 + [shape(16, 4, 8, 256)] * 2,
        [SMEM] + [VMEM] * 3,
        [pltpu.VMEM((1152, 256), BF16), pltpu.VMEM((256, 256), F32)],
        flops=6 * 256 * 384 * 1024,
        limit=12,
    )(tab, keep, other, spread)
    term = mine + swap_core(yours)

    term = lax.all_to_all(term, PLANE, 0, 0)
    parts, term = lax.optimization_barrier((parts, term))
    parts = [parts[0]] + [shift_x(parts[k], k) for k in (1, 2, 3)]
    total = jnp.sum(term, axis=0)
    total = lax.all_to_all(jnp.broadcast_to(total[None], (8, 4, 8, 256)), "z", 0, 0)
    *parts, total = lax.optimization_barrier((*parts, total))
    parts = call(sum_body, shape(2, 4, 48, 256), [VMEM] * 4)(*parts)
    part = flip_y(parts[1])
    total = jnp.sum(total, axis=0)
    total = lax.all_to_all(jnp.broadcast_to(total[None], (16, 4, 8, 256)), PLANE, 0, 0)
    part, total = lax.optimization_barrier((part, total))
    shares = parts[0] + part
    diag = call(last_body, shape(4, 256, 256), [SMEM] + [VMEM] * 3)(
        tab, total, swap_core(total), dinv
    )
    return shares.reshape(4, 3, 1, 16, 256), diag


def solution(mesh):
    fine = Mesh(mesh.devices.reshape(2, 8, 2, 4, 2), AXES)
    rows, columns = ("y_lo", "z"), ("y_hi", "x", "core")
    return jax.shard_map(
        process,
        mesh=fine,
        in_specs=(
            P(None, rows, None, None, columns, None),
            P(None, None, rows, columns, None),
            P(),
            P(),
            P(),
        ),
        out_specs=(P(None, None, rows, columns, None), P()),
        check_vma=False,
    )
```

```python
import functools

import jax
import jax.numpy as jnp
from jax import lax
from jax.experimental import pallas as pl
from jax.experimental.pallas import tpu as pltpu
from jax.sharding import Mesh, PartitionSpec as P


F32 = jnp.float32
BF16 = jnp.bfloat16
HIGHEST = lax.Precision.HIGHEST

AXES = ("y_lo", "z", "y_hi", "x", "core")
PLANE = ("y_lo", "y_hi", "x")
LANDING = (0, 4, 1, 6, 2, 7, 3, 5)
SOURCE = tuple(LANDING.index(d) for d in range(8))
SMEM = pl.BlockSpec(memory_space=pltpu.SMEM)
VMEM = pl.BlockSpec(memory_space=pltpu.VMEM)
HBM = pl.BlockSpec(memory_space=pltpu.MemorySpace.HBM)
DMA = pltpu.SemaphoreType.DMA


def to_columns(v):
    pairs = []
    for p in range(16):
        for q in range(16):
            row = (q // 8) * 8 + (p % 8 + LANDING[q % 8]) % 8
            pairs.append((p * 16 + q, row * 16 + p))
    return lax.ppermute(v, AXES, pairs)


def swap_y(v):
    return lax.ppermute(v, "y_lo", [(0, 1), (1, 0)])


def shift_z(v, d):
    return lax.ppermute(v, "z", [(p, (p + d) % 8) for p in range(8)])


def swap_core(v):
    return lax.ppermute(v, "core", [(0, 1), (1, 0)])


def flip_y(v):
    return lax.ppermute(v, "y_hi", [(0, 1), (1, 0)])


def shift_x(v, d):
    return lax.ppermute(v, "x", [(p, (p + d) % 4) for p in range(4)])


def call(body, outs, specs, scratch=(), flops=0, limit=8):
    return pl.pallas_call(
        body,
        out_shape=outs,
        in_specs=specs,
        out_specs=jax.tree.map(lambda _: VMEM, outs),
        scratch_shapes=list(scratch),
        compiler_params=pltpu.CompilerParams(vmem_limit_bytes=limit << 20),
        cost_estimate=pl.CostEstimate(flops=flops, transcendentals=0, bytes_accessed=4 << 20),
    )


def shape(*dims, dtype=F32):
    return jax.ShapeDtypeStruct(dims, dtype)


def split_two(v):
    high = v.astype(BF16)
    return high, (v - high.astype(F32)).astype(BF16)


def fetched_body(tab, *refs):
    sources, out, targets, sems = refs[:3], refs[3], refs[4:7], refs[7:]
    copies = [pltpu.make_async_copy(*c) for c in zip(sources, targets, sems)]
    for c in copies:
        c.start()
    for c in copies:
        c.wait()
    panel_body(0, tab, *targets, out)


def panel_body(which, tab, present, panel, inverse, out):
    p = tab[which]
    for s in range(4):
        value = jnp.dot(panel[s], inverse[s], precision=HIGHEST, preferred_element_type=F32)
        for i in range(3):
            live = present[s, i * 16 + p].astype(F32)
            out[s, i * 16 : i * 16 + 16] = value[i * 16 : i * 16 + 16] * live


def matrix_body(tab, source, out, a, *sems):
    core, x, yh = tab[2], tab[3], tab[5]
    copies = []
    for i in range(3):
        at = pl.ds(i * 1536, 1536)
        copies.append(pltpu.make_async_copy(source.at[at], a.at[at], sems[i]))
        copies[i].start()
    for i in range(3):
        copies[i].wait()

        @pl.loop(0, 16)
        def _(g):
            place = (yh + g) % 2 * 4 + (x + g // 2) % 4
            start = place * 32 + ((core + g // 8) % 2) * 16
            at = pl.ds(pl.multiple_of(g * 48 + i * 16, 16), 16)
            for j in range(3):
                for half in range(2):
                    block = a[pl.ds(((i * 256 + start) * 3 + j) * 2 + half, 16, stride=6), :]
                    h, l = split_two(-block)
                    for term, part in enumerate((h, l, h)):
                        col = term * 384 + j * 128
                        out[half, at, col : col + 128] = part


def product_body(flip, sides, tab, matrix, *refs):
    n = len(sides)
    before, pieces = (refs[:n], refs[n : n + 9]) if flip else (None, refs[:9])
    outs, held = refs[-n - 1 : -1], refs[-1]
    half = (tab[1] + flip) % 2

    def put(block, d):
        start = pl.multiple_of(tab[8 + d % 8], 16)
        h, l = split_two(block)
        for i in range(3):
            for term, part in enumerate((l, h, h)):
                held[pl.ds(term * 384 + i * 128 + start, 16), :] = part[i * 16 : i * 16 + 16]

    @pl.loop(0, 4)
    def _(s):
        for ref, d in zip(pieces[:7], (0, 1, 2, 3, -1, -2, -3)):
            put(ref[s], d)

        @pl.when(s < 2)
        def _():
            put(pieces[7][s % 2], 4)

        @pl.when(s >= 2)
        def _():
            put(pieces[8][s % 2], 4)

        for n, c in enumerate(sides):
            value = jnp.dot(
                matrix[half, c * 384 : c * 384 + 384, :], held[...], preferred_element_type=F32
            )
            for k in range(8):
                part = value[k * 48 : k * 48 + 48]
                outs[n][k, s] = part if before is None else before[n][k, s] + part


def spread_body(*refs):
    rows, out, held = refs[:2], refs[2], refs[3]

    @pl.loop(0, 4)
    def _(s):
        for k in range(8):
            held[k * 48 : k * 48 + 48, :] = rows[k % 2][k // 2, s]
        h, l = split_two(held[...].T)
        for term, part in enumerate((h, l, h)):
            out[s, :, term * 384 : term * 384 + 384] = part


def pair_body(tab, keep, other, spread, *refs):
    parts, (mine, yours, held, value) = refs[:4], refs[4:]
    core = tab[2]

    @pl.loop(0, 4)
    def _(s):
        for k in range(8):
            part = keep[k, s] + other[k, s]
            parts[k // 2][k % 2, s] = part
            h, l = split_two(part)
            for term, piece in enumerate((l, h, h)):
                at = term * 384 + k * 48
                held[at : at + 48, :] = piece
        value[...] = jnp.dot(spread[s], held[...], preferred_element_type=F32)
        for out, base in ((mine, core * 128), (yours, 128 - core * 128)):
            for e in range(16):
                out[e, s] = value[pl.ds(pl.multiple_of(base + e * 8, 8), 8), :]


def sum_body(*refs):
    value = refs[0][...]
    for r in refs[1:-1]:
        value = value + r[...]
    refs[-1][...] = value


def last_body(tab, own, other, dinv, out):
    core = tab[2]
    for k, r in enumerate((own, other)):
        base = pl.multiple_of(((core + k) % 2) * 128, 128)
        for s in range(4):
            for e in range(16):
                at = pl.ds(base + e * 8, 8)
                out[s, at, :] = dinv[s, at, :] - r[e, s]


def process(ainv, panel, diag_inv, dinv, present):
    yl, z, yh, x, core = (lax.axis_index(a) for a in AXES)
    place = jnp.arange(8, dtype=jnp.int32)
    landed = (z - place - (x * 2 + core)) % 8
    source = sum(jnp.where(landed == d, SOURCE[d], 0) for d in range(8))
    head = jnp.stack([yl * 8 + z, yl, core, x, z, yh, yh * 8 + x * 2 + core, yh]).astype(jnp.int32)
    tab = jnp.concatenate([head, (source * 16).astype(jnp.int32)])

    panel = panel.reshape(4, 48, 256)

    arrived = to_columns(panel)
    lhat = call(
        fetched_body,
        shape(4, 48, 256),
        [SMEM] + [HBM] * 3,
        [
            pltpu.SMEM((4, 48), jnp.int32),
            pltpu.VMEM((4, 48, 256), F32),
            pltpu.VMEM((4, 256, 256), F32),
            DMA, DMA, DMA,
        ],
    )(tab, present, panel, diag_inv)
    near = jnp.stack([lhat] + [shift_x(lhat, -d) for d in (1, 2, 3)])
    matrix = call(
        matrix_body,
        shape(2, 768, 1152, dtype=BF16),
        [SMEM, HBM],
        [pltpu.VMEM((4608, 128), F32), DMA, DMA, DMA],
    )(tab, ainv.reshape(4608, 128))
    arrived, matrix = lax.optimization_barrier((arrived, matrix))
    own = call(
        functools.partial(panel_body, 6), shape(4, 48, 256), [SMEM, SMEM, VMEM, VMEM]
    )(tab, present, arrived, diag_inv)
    far = flip_y(near)
    spread = call(
        spread_body,
        shape(4, 256, 1152, dtype=BF16),
        [VMEM] * 2,
        [pltpu.VMEM((384, 256), F32)],
    )(near, far)

    chains = []
    for first in (own, swap_y(own)):
        a1, b1 = shift_z(first, 1), shift_z(first, -1)
        a2, b2 = shift_z(a1, 1), shift_z(b1, -1)
        a3, b3 = shift_z(a2, 1), shift_z(b2, -1)
        a4, b4 = shift_z(a3[:2], 1), shift_z(b3[2:], -1)
        chains.append((first, a1, a2, a3, b1, b2, b3, a4, b4))

    def product(flip, sides, *before):
        return call(
            functools.partial(product_body, flip, sides),
            [shape(8, 4, 48, 256)] * len(sides),
            [SMEM] + [VMEM] * (1 + len(before) + 9),
            [pltpu.VMEM((1152, 256), BF16)],
            flops=3 * 768 * 384 * 1024 * len(sides),
            limit=12,
        )(tab, matrix, *before, *chains[flip])

    keep, send = product(0, (0, 1))
    keep, send, spread = lax.optimization_barrier((keep, send, spread))
    (send,) = product(1, (1,), send)
    other = swap_core(send)
    (keep,) = product(1, (0,), keep)
    *parts, mine, yours = call(
        pair_body,
        [shape(2, 4, 48, 256)] * 4 + [shape(16, 4, 8, 256)] * 2,
        [SMEM] + [VMEM] * 3,
        [pltpu.VMEM((1152, 256), BF16), pltpu.VMEM((256, 256), F32)],
        flops=6 * 256 * 384 * 1024,
        limit=12,
    )(tab, keep, other, spread)
    parts = [parts[0]] + [shift_x(parts[k], k) for k in (1, 2, 3)]
    parts = call(sum_body, shape(2, 4, 48, 256), [VMEM] * 4)(*parts)
    part = flip_y(parts[1])
    shares = parts[0] + part

    term = mine + swap_core(yours)
    total = jnp.sum(lax.all_to_all(term, PLANE, 0, 0), axis=0)
    total = lax.all_to_all(jnp.broadcast_to(total[None], (8, 4, 8, 256)), "z", 0, 0)
    total = jnp.sum(total, axis=0)
    total = lax.all_to_all(jnp.broadcast_to(total[None], (16, 4, 8, 256)), PLANE, 0, 0)
    diag = call(last_body, shape(4, 256, 256), [SMEM] + [VMEM] * 3)(
        tab, total, swap_core(total), dinv
    )
    return shares.reshape(4, 3, 1, 16, 256), diag


def solution(mesh):
    fine = Mesh(mesh.devices.reshape(2, 8, 2, 4, 2), AXES)
    rows, columns = ("y_lo", "z"), ("y_hi", "x", "core")
    return jax.shard_map(
        process,
        mesh=fine,
        in_specs=(
            P(None, rows, None, None, columns, None),
            P(None, None, rows, columns, None),
            P(),
            P(),
            P(),
        ),
        out_specs=(P(None, None, rows, columns, None), P()),
        check_vma=False,
    )
```

```python
import functools

import jax
import jax.numpy as jnp
from jax import lax
from jax.experimental import pallas as pl
from jax.experimental.pallas import tpu as pltpu
from jax.sharding import Mesh, PartitionSpec as P


F32 = jnp.float32
BF16 = jnp.bfloat16
HIGHEST = lax.Precision.HIGHEST

AXES = ("y_lo", "z", "y_hi", "x", "core")
PLANE = ("y_lo", "y_hi", "x")
LANDING = (0, 4, 1, 6, 2, 7, 3, 5)
SOURCE = tuple(LANDING.index(d) for d in range(8))
STEPS = (0, 1, 2, 3, -1, -2, -3, 4)
SMEM = pl.BlockSpec(memory_space=pltpu.SMEM)
VMEM = pl.BlockSpec(memory_space=pltpu.VMEM)
HBM = pl.BlockSpec(memory_space=pltpu.MemorySpace.HBM)
DMA = pltpu.SemaphoreType.DMA


def to_columns(v):
    pairs = []
    for p in range(16):
        for q in range(16):
            row = (q // 8) * 8 + (p % 8 + LANDING[q % 8]) % 8
            pairs.append((p * 16 + q, row * 16 + p))
    return lax.ppermute(v, AXES, pairs)


def swap_y(v):
    return lax.ppermute(v, "y_lo", [(0, 1), (1, 0)])


def shift_z(v, d):
    return lax.ppermute(v, "z", [(p, (p + d) % 8) for p in range(8)])


def swap_core(v):
    return lax.ppermute(v, "core", [(0, 1), (1, 0)])


def flip_y(v):
    return lax.ppermute(v, "y_hi", [(0, 1), (1, 0)])


def shift_x(v, d):
    return lax.ppermute(v, "x", [(p, (p + d) % 4) for p in range(4)])


def call(body, outs, specs, scratch=(), flops=0, limit=8):
    return pl.pallas_call(
        body,
        out_shape=outs,
        in_specs=specs,
        out_specs=jax.tree.map(lambda _: VMEM, outs),
        scratch_shapes=list(scratch),
        compiler_params=pltpu.CompilerParams(vmem_limit_bytes=limit << 20),
        cost_estimate=pl.CostEstimate(flops=flops, transcendentals=0, bytes_accessed=4 << 20),
    )


def in_hbm(v):
    return pltpu.with_memory_space_constraint(v, pltpu.MemorySpace.HBM)


def shape(*dims, dtype=F32):
    return jax.ShapeDtypeStruct(dims, dtype)


def split_two(v):
    high = v.astype(BF16)
    return high, (v - high.astype(F32)).astype(BF16)


def fetched_body(tab, *refs):
    sources, out, targets, sems = refs[:3], refs[3], refs[4:7], refs[7:]
    copies = [pltpu.make_async_copy(*c) for c in zip(sources, targets, sems)]
    for c in copies:
        c.start()
    for c in copies:
        c.wait()
    panel_body(0, tab, *targets, out)


def panel_body(which, tab, present, panel, inverse, out):
    p = tab[which]
    for s in range(4):
        value = jnp.dot(panel[s], inverse[s], precision=HIGHEST, preferred_element_type=F32)
        for i in range(3):
            live = present[s, i * 16 + p].astype(F32)
            out[s, i * 16 : i * 16 + 16] = value[i * 16 : i * 16 + 16] * live


def matrix_body(tab, source, out, a, *sems):
    core, x, yh = tab[2], tab[3], tab[5]
    copies = []
    for i in range(3):
        at = pl.ds(i * 1536, 1536)
        copies.append(pltpu.make_async_copy(source.at[at], a.at[at], sems[i]))
        copies[i].start()
    for i in range(3):
        copies[i].wait()

        @pl.loop(0, 16)
        def _(g):
            place = (yh + g) % 2 * 4 + (x + g // 2) % 4
            start = place * 32 + ((core + g // 8) % 2) * 16
            at = pl.ds(pl.multiple_of(g * 48 + i * 16, 16), 16)
            for j in range(3):
                for half in range(2):
                    block = a[pl.ds(((i * 256 + start) * 3 + j) * 2 + half, 16, stride=6), :]
                    h, l = split_two(-block)
                    for term, part in enumerate((h, l, h)):
                        col = term * 768 + half * 384 + j * 128
                        out[at, col : col + 128] = part


def product_body(side, tab, matrix, *refs):
    pieces, out, held = refs[:16], refs[16], refs[17]

    @pl.loop(0, 4)
    def _(s):
        for n, ref in enumerate(pieces):
            half = (tab[1] + n // 8) % 2
            start = pl.multiple_of(half * 384 + tab[8 + STEPS[n % 8] % 8], 16)
            h, l = split_two(ref[s])
            for i in range(3):
                for term, part in enumerate((l, h, h)):
                    at = pl.ds(term * 768 + i * 128 + start, 16)
                    held[at, :] = part[i * 16 : i * 16 + 16]
        value = jnp.dot(
            matrix[side * 384 : side * 384 + 384, :], held[...], preferred_element_type=F32
        )
        for k in range(8):
            out[k, s] = value[k * 48 : k * 48 + 48]


def spread_body(*refs):
    rows, out, held = refs[:2], refs[2], refs[3]

    @pl.loop(0, 4)
    def _(s):
        for k in range(8):
            held[k * 48 : k * 48 + 48, :] = rows[k % 2][k // 2, s]
        h, l = split_two(held[...].T)
        for term, part in enumerate((h, l, h)):
            out[s, :, term * 384 : term * 384 + 384] = part


def pair_body(tab, keep, other, spread, *refs):
    parts, (mine, yours, held, value) = refs[:4], refs[4:]
    core = tab[2]

    @pl.loop(0, 4)
    def _(s):
        for k in range(8):
            part = keep[k, s] + other[k, s]
            parts[k // 2][k % 2, s] = part
            h, l = split_two(part)
            for term, piece in enumerate((l, h, h)):
                at = term * 384 + k * 48
                held[at : at + 48, :] = piece
        value[...] = jnp.dot(spread[s], held[...], preferred_element_type=F32)
        for out, base in ((mine, core * 128), (yours, 128 - core * 128)):
            for e in range(16):
                out[e, s] = value[pl.ds(pl.multiple_of(base + e * 8, 8), 8), :]


def sum_body(a, b, c, d, mine, yours):
    for k, out in enumerate((mine, yours)):
        out[...] = (a[k] + b[k]) + (c[k] + d[k])


def last_body(tab, own, other, dinv, out):
    core = tab[2]
    for k, r in enumerate((own, other)):
        base = pl.multiple_of(((core + k) % 2) * 128, 128)
        for s in range(4):
            for e in range(16):
                at = pl.ds(base + e * 8, 8)
                out[s, at, :] = dinv[s, at, :] - r[e, s]


def process(ainv, panel, diag_inv, dinv, present):
    yl, z, yh, x, core = (lax.axis_index(a) for a in AXES)
    place = jnp.arange(8, dtype=jnp.int32)
    landed = (z - place - (x * 2 + core)) % 8
    source = sum(jnp.where(landed == d, SOURCE[d], 0) for d in range(8))
    head = jnp.stack([yl * 8 + z, yl, core, x, z, yh, yh * 8 + x * 2 + core, yh]).astype(jnp.int32)
    tab = jnp.concatenate([head, (source * 16).astype(jnp.int32)])

    panel = panel.reshape(4, 48, 256)

    arrived = to_columns(panel)
    lhat = call(
        fetched_body,
        shape(4, 48, 256),
        [SMEM] + [HBM] * 3,
        [
            pltpu.SMEM((4, 48), jnp.int32),
            pltpu.VMEM((4, 48, 256), F32),
            pltpu.VMEM((4, 256, 256), F32),
            DMA, DMA, DMA,
        ],
    )(tab, in_hbm(present), in_hbm(panel), in_hbm(diag_inv))
    near = jnp.stack([lhat] + [shift_x(lhat, -d) for d in (1, 2, 3)])
    matrix = call(
        matrix_body,
        shape(768, 2304, dtype=BF16),
        [SMEM, HBM],
        [pltpu.VMEM((4608, 128), F32), DMA, DMA, DMA],
    )(tab, in_hbm(ainv.reshape(4608, 128)))
    arrived, matrix = lax.optimization_barrier((arrived, matrix))
    own = call(
        functools.partial(panel_body, 6), shape(4, 48, 256), [SMEM, SMEM, VMEM, VMEM]
    )(tab, present, arrived, diag_inv)
    far = flip_y(near)
    spread = call(
        spread_body,
        shape(4, 256, 1152, dtype=BF16),
        [VMEM] * 2,
        [pltpu.VMEM((384, 256), F32)],
    )(near, far)

    pieces = []
    for flip, first in enumerate((own, swap_y(own))):
        ahead, back = [first], [first]
        for _ in range(3):
            ahead.append(shift_z(ahead[-1], 1))
            back.append(shift_z(back[-1], -1))
        last = shift_z(back[-1], -1) if flip else shift_z(ahead[-1], 1)
        pieces += ahead + back[1:] + [last]

    def product(side):
        return call(
            functools.partial(product_body, side),
            shape(8, 4, 48, 256),
            [SMEM] + [VMEM] * 17,
            [pltpu.VMEM((2304, 256), BF16)],
            flops=6 * 384 * 768 * 1024,
            limit=12,
        )(tab, matrix, *pieces)

    send = product(1)
    send, spread = lax.optimization_barrier((send, spread))
    other = swap_core(send)
    keep = product(0)
    *parts, mine, yours = call(
        pair_body,
        [shape(2, 4, 48, 256)] * 4 + [shape(16, 4, 8, 256)] * 2,
        [SMEM] + [VMEM] * 3,
        [pltpu.VMEM((1152, 256), BF16), pltpu.VMEM((256, 256), F32)],
        flops=6 * 256 * 384 * 1024,
        limit=12,
    )(tab, keep, other, spread)
    parts = [parts[0]] + [shift_x(parts[k], k) for k in (1, 2, 3)]
    part, far = call(sum_body, [shape(4, 48, 256)] * 2, [VMEM] * 4)(*parts)
    far = flip_y(far)

    term = mine + swap_core(yours)
    total = jnp.sum(lax.all_to_all(term, PLANE, 0, 0), axis=0)
    total = lax.all_to_all(jnp.broadcast_to(total[None], (8, 4, 8, 256)), "z", 0, 0)
    total = jnp.sum(total, axis=0)
    total = lax.all_to_all(jnp.broadcast_to(total[None], (16, 4, 8, 256)), PLANE, 0, 0)
    total, far = lax.optimization_barrier((total, far))
    shares = part + far
    diag = call(last_body, shape(4, 256, 256), [SMEM] + [VMEM] * 3)(
        tab, total, swap_core(total), dinv
    )
    return shares.reshape(4, 3, 1, 16, 256), diag


def solution(mesh):
    fine = Mesh(mesh.devices.reshape(2, 8, 2, 4, 2), AXES)
    rows, columns = ("y_lo", "z"), ("y_hi", "x", "core")
    return jax.shard_map(
        process,
        mesh=fine,
        in_specs=(
            P(None, rows, None, None, columns, None),
            P(None, None, rows, columns, None),
            P(),
            P(),
            P(),
        ),
        out_specs=(P(None, None, rows, columns, None), P()),
        check_vma=False,
    )
```

```python
import functools

import jax
import jax.numpy as jnp
from jax import lax
from jax.experimental import pallas as pl
from jax.experimental.pallas import tpu as pltpu
from jax.sharding import Mesh, PartitionSpec as P


F32 = jnp.float32
BF16 = jnp.bfloat16
HIGHEST = lax.Precision.HIGHEST

AXES = ("y_lo", "z", "y_hi", "x", "core")
PLANE = ("y_lo", "y_hi", "x")
LANDING = (0, 4, 1, 6, 2, 7, 3, 5)
SOURCE = tuple(LANDING.index(d) for d in range(8))
STEPS = (0, 1, 2, 3, -1, -2, -3, 4)
SMEM = pl.BlockSpec(memory_space=pltpu.SMEM)
VMEM = pl.BlockSpec(memory_space=pltpu.VMEM)
HBM = pl.BlockSpec(memory_space=pltpu.MemorySpace.HBM)
DMA = pltpu.SemaphoreType.DMA


def to_columns(v):
    pairs = []
    for p in range(16):
        for q in range(16):
            row = (q // 8) * 8 + (p % 8 + LANDING[q % 8]) % 8
            pairs.append((p * 16 + q, row * 16 + p))
    return lax.ppermute(v, AXES, pairs)


def swap_y(v):
    return lax.ppermute(v, "y_lo", [(0, 1), (1, 0)])


def shift_z(v, d):
    return lax.ppermute(v, "z", [(p, (p + d) % 8) for p in range(8)])


def swap_core(v):
    return lax.ppermute(v, "core", [(0, 1), (1, 0)])


def flip_y(v):
    return lax.ppermute(v, "y_hi", [(0, 1), (1, 0)])


def shift_x(v, d):
    return lax.ppermute(v, "x", [(p, (p + d) % 4) for p in range(4)])


def call(body, outs, specs, scratch=(), flops=0, limit=8):
    return pl.pallas_call(
        body,
        out_shape=outs,
        in_specs=specs,
        out_specs=jax.tree.map(lambda _: VMEM, outs),
        scratch_shapes=list(scratch),
        compiler_params=pltpu.CompilerParams(vmem_limit_bytes=limit << 20),
        cost_estimate=pl.CostEstimate(flops=flops, transcendentals=0, bytes_accessed=4 << 20),
    )


def in_hbm(v):
    return pltpu.with_memory_space_constraint(v, pltpu.MemorySpace.HBM)


def shape(*dims, dtype=F32):
    return jax.ShapeDtypeStruct(dims, dtype)


def split_two(v):
    high = v.astype(BF16)
    return high, (v - high.astype(F32)).astype(BF16)


def panel_body(tab, present, panel, inverse, out, fetched, live, rows, *sems):
    copies = [
        pltpu.make_async_copy(*c)
        for c in zip((present, panel, inverse), (live, rows, fetched), sems)
    ]
    for c in copies:
        c.start()
    copies[1].wait()
    copies[2].wait()
    multiply(rows, fetched, out)
    copies[0].wait()
    clear(tab[0], live, out)


def own_body(tab, present, rows, inverse, out, live, sem):
    copy = pltpu.make_async_copy(present, live, sem)
    copy.start()
    multiply(rows, inverse, out)
    copy.wait()
    clear(tab[6], live, out)


def multiply(rows, inverse, out):
    for s in range(4):
        out[s] = jnp.dot(rows[s], inverse[s], precision=HIGHEST, preferred_element_type=F32)


def clear(p, live, out):
    for s in range(4):
        for i in range(3):
            at = slice(i * 16, i * 16 + 16)
            out[s, at] = out[s, at] * live[s, i * 16 + p].astype(F32)


def matrix_body(tab, source, out, a, *sems):
    core, x, yh = tab[2], tab[3], tab[5]
    copies = []
    for i in range(3):
        at = pl.ds(i * 1536, 1536)
        copies.append(pltpu.make_async_copy(source.at[at], a.at[at], sems[i]))
        copies[i].start()
    for i in range(3):
        copies[i].wait()

        @pl.loop(0, 16)
        def _(g):
            place = (yh + g) % 2 * 4 + (x + g // 2) % 4
            start = place * 32 + ((core + g // 8) % 2) * 16
            at = pl.ds(pl.multiple_of(g * 48 + i * 16, 16), 16)
            for j in range(3):
                for half in range(2):
                    block = a[pl.ds(((i * 256 + start) * 3 + j) * 2 + half, 16, stride=6), :]
                    h, l = split_two(-block)
                    for term, part in enumerate((h, l, h)):
                        col = term * 768 + half * 384 + j * 128
                        out[at, col : col + 128] = part


def product_body(side, tab, matrix, *refs):
    pieces, out, held = refs[:16], refs[16], refs[17]

    @pl.loop(0, 4)
    def _(s):
        for n, ref in enumerate(pieces):
            half = (tab[1] + n // 8) % 2
            start = pl.multiple_of(half * 384 + tab[8 + STEPS[n % 8] % 8], 16)
            h, l = split_two(ref[s])
            for i in range(3):
                for term, part in enumerate((l, h, h)):
                    at = pl.ds(term * 768 + i * 128 + start, 16)
                    held[at, :] = part[i * 16 : i * 16 + 16]
        value = jnp.dot(
            matrix[side * 384 : side * 384 + 384, :], held[...], preferred_element_type=F32
        )
        for k in range(8):
            out[k, s] = value[k * 48 : k * 48 + 48]


def spread_body(*refs):
    rows, out, held = refs[:2], refs[2], refs[3]

    @pl.loop(0, 4)
    def _(s):
        for k in range(8):
            held[k * 48 : k * 48 + 48, :] = rows[k % 2][k // 2, s]
        h, l = split_two(held[...].T)
        for term, part in enumerate((h, l, h)):
            out[s, :, term * 384 : term * 384 + 384] = part


def pair_body(tab, keep, other, spread, *refs):
    parts, (mine, yours, held, value) = refs[:4], refs[4:]
    core = tab[2]

    @pl.loop(0, 4)
    def _(s):
        for k in range(8):
            part = keep[k, s] + other[k, s]
            parts[k // 2][k % 2, s] = part
            h, l = split_two(part)
            for term, piece in enumerate((l, h, h)):
                at = term * 384 + k * 48
                held[at : at + 48, :] = piece
        value[...] = jnp.dot(spread[s], held[...], preferred_element_type=F32)
        for out, base in ((mine, core * 128), (yours, 128 - core * 128)):
            for e in range(16):
                out[e, s] = value[pl.ds(pl.multiple_of(base + e * 8, 8), 8), :]


def sum_body(a, b, c, d, mine, yours):
    for k, out in enumerate((mine, yours)):
        out[...] = (a[k] + b[k]) + (c[k] + d[k])


def last_body(tab, own, other, dinv, out):
    core = tab[2]
    for k, r in enumerate((own, other)):
        base = pl.multiple_of(((core + k) % 2) * 128, 128)
        for s in range(4):
            for e in range(16):
                at = pl.ds(base + e * 8, 8)
                out[s, at, :] = dinv[s, at, :] - r[e, s]


def process(ainv, panel, diag_inv, dinv, present):
    yl, z, yh, x, core = (lax.axis_index(a) for a in AXES)
    place = jnp.arange(8, dtype=jnp.int32)
    landed = (z - place - (x * 2 + core)) % 8
    source = sum(jnp.where(landed == d, SOURCE[d], 0) for d in range(8))
    head = jnp.stack([yl * 8 + z, yl, core, x, z, yh, yh * 8 + x * 2 + core, yh]).astype(jnp.int32)
    tab = jnp.concatenate([head, (source * 16).astype(jnp.int32)])

    panel = panel.reshape(4, 48, 256)

    arrived = to_columns(panel)
    lhat, inverse = call(
        panel_body,
        [shape(4, 48, 256), shape(4, 256, 256)],
        [SMEM] + [HBM] * 3,
        [pltpu.SMEM((4, 48), jnp.int32), pltpu.VMEM((4, 48, 256), F32), DMA, DMA, DMA],
    )(tab, in_hbm(present), in_hbm(panel), in_hbm(diag_inv))
    near = [lhat] + [shift_x(lhat, -d) for d in (1, 2, 3)]
    matrix = call(
        matrix_body,
        shape(768, 2304, dtype=BF16),
        [SMEM, HBM],
        [pltpu.VMEM((4608, 128), F32), DMA, DMA, DMA],
    )(tab, in_hbm(ainv.reshape(4608, 128)))
    own = call(
        own_body,
        shape(4, 48, 256),
        [SMEM, HBM, VMEM, VMEM],
        [pltpu.SMEM((4, 48), jnp.int32), DMA],
    )(tab, in_hbm(present), arrived, inverse)
    pieces = []
    mate = swap_y(own)
    for flip, first in enumerate((own, mate)):
        ahead, back = [first], [first]
        for _ in range(3):
            ahead.append(shift_z(ahead[-1], 1))
            back.append(shift_z(back[-1], -1))
        last = shift_z(back[-1], -1) if flip else shift_z(ahead[-1], 1)
        pieces += ahead + back[1:] + [last]

    near = jnp.stack(near)
    far = flip_y(near)
    spread = call(
        spread_body,
        shape(4, 256, 1152, dtype=BF16),
        [VMEM] * 2,
        [pltpu.VMEM((384, 256), F32)],
    )(near, far)

    def product(side):
        return call(
            functools.partial(product_body, side),
            shape(8, 4, 48, 256),
            [SMEM] + [VMEM] * 17,
            [pltpu.VMEM((2304, 256), BF16)],
            flops=6 * 384 * 768 * 1024,
            limit=12,
        )(tab, matrix, *pieces)

    send = product(1)
    send, spread = lax.optimization_barrier((send, spread))
    other = swap_core(send)
    keep = product(0)
    *parts, mine, yours = call(
        pair_body,
        [shape(2, 4, 48, 256)] * 4 + [shape(16, 4, 8, 256)] * 2,
        [SMEM] + [VMEM] * 3,
        [pltpu.VMEM((1152, 256), BF16), pltpu.VMEM((256, 256), F32)],
        flops=6 * 256 * 384 * 1024,
        limit=12,
    )(tab, keep, other, spread)
    parts = [parts[0]] + [shift_x(parts[k], k) for k in (1, 2, 3)]
    part, far = call(sum_body, [shape(4, 48, 256)] * 2, [VMEM] * 4)(*parts)
    far = flip_y(far)

    term = mine + swap_core(yours)
    total = jnp.sum(lax.all_to_all(term, PLANE, 0, 0), axis=0)
    total = lax.all_to_all(jnp.broadcast_to(total[None], (8, 4, 8, 256)), "z", 0, 0)
    total = jnp.sum(total, axis=0)
    total = lax.all_to_all(jnp.broadcast_to(total[None], (16, 4, 8, 256)), PLANE, 0, 0)
    shares = part + far
    diag = call(last_body, shape(4, 256, 256), [SMEM] + [VMEM] * 3)(
        tab, total, swap_core(total), dinv
    )
    return shares.reshape(4, 3, 1, 16, 256), diag


def solution(mesh):
    fine = Mesh(mesh.devices.reshape(2, 8, 2, 4, 2), AXES)
    rows, columns = ("y_lo", "z"), ("y_hi", "x", "core")
    return jax.shard_map(
        process,
        mesh=fine,
        in_specs=(
            P(None, rows, None, None, columns, None),
            P(None, None, rows, columns, None),
            P(),
            P(),
            P(),
        ),
        out_specs=(P(None, None, rows, columns, None), P()),
        check_vma=False,
    )
```

```python
import functools

import jax
import jax.numpy as jnp
from jax import lax
from jax.experimental import pallas as pl
from jax.experimental.pallas import tpu as pltpu
from jax.sharding import Mesh, PartitionSpec as P


F32 = jnp.float32
BF16 = jnp.bfloat16
HIGHEST = lax.Precision.HIGHEST

AXES = ("y_lo", "z", "y_hi", "x", "core")
PLANE = ("y_lo", "y_hi", "x")
LANDING = (0, 4, 1, 6, 2, 7, 3, 5)
SOURCE = tuple(LANDING.index(d) for d in range(8))
STEPS = (0, 1, 2, 3, -1, -2, -3)
SMEM = pl.BlockSpec(memory_space=pltpu.SMEM)
VMEM = pl.BlockSpec(memory_space=pltpu.VMEM)
HBM = pl.BlockSpec(memory_space=pltpu.MemorySpace.HBM)
DMA = pltpu.SemaphoreType.DMA


def to_columns(v):
    pairs = []
    for p in range(16):
        for q in range(16):
            row = (q // 8) * 8 + (p % 8 + LANDING[q % 8]) % 8
            pairs.append((p * 16 + q, row * 16 + p))
    return lax.ppermute(v, AXES, pairs)


def swap_y(v):
    return lax.ppermute(v, "y_lo", [(0, 1), (1, 0)])


def shift_z(v, d):
    return lax.ppermute(v, "z", [(p, (p + d) % 8) for p in range(8)])


def swap_core(v):
    return lax.ppermute(v, "core", [(0, 1), (1, 0)])


def flip_y(v):
    return lax.ppermute(v, "y_hi", [(0, 1), (1, 0)])


def shift_x(v, d):
    return lax.ppermute(v, "x", [(p, (p + d) % 4) for p in range(4)])


def call(body, outs, specs, scratch=(), flops=0, limit=8):
    return pl.pallas_call(
        body,
        out_shape=outs,
        in_specs=specs,
        out_specs=jax.tree.map(lambda _: VMEM, outs),
        scratch_shapes=list(scratch),
        compiler_params=pltpu.CompilerParams(vmem_limit_bytes=limit << 20),
        cost_estimate=pl.CostEstimate(flops=flops, transcendentals=0, bytes_accessed=4 << 20),
    )


def in_hbm(v):
    return pltpu.with_memory_space_constraint(v, pltpu.MemorySpace.HBM)


def shape(*dims, dtype=F32):
    return jax.ShapeDtypeStruct(dims, dtype)


def split_two(v):
    high = v.astype(BF16)
    return high, (v - high.astype(F32)).astype(BF16)


def panel_body(tab, present, panel, inverse, out, fetched, live, rows, *sems):
    copies = [
        pltpu.make_async_copy(*c)
        for c in zip((present, panel, inverse), (live, rows, fetched), sems)
    ]
    for c in copies:
        c.start()
    copies[1].wait()
    copies[2].wait()
    multiply(rows, fetched, out)
    copies[0].wait()
    clear(tab[0], live, out)


def own_body(tab, present, rows, inverse, out, live, sem):
    copy = pltpu.make_async_copy(present, live, sem)
    copy.start()
    multiply(rows, inverse, out)
    copy.wait()
    clear(tab[6], live, out)


def multiply(rows, inverse, out):
    for s in range(4):
        out[s] = jnp.dot(rows[s], inverse[s], precision=HIGHEST, preferred_element_type=F32)


def clear(p, live, out):
    for s in range(4):
        for i in range(3):
            at = slice(i * 16, i * 16 + 16)
            out[s, at] = out[s, at] * live[s, i * 16 + p].astype(F32)


def matrix_body(tab, source, out, a, *sems):
    core, x, yh = tab[2], tab[3], tab[5]
    copies = []
    for i in range(3):
        at = pl.ds(i * 1536, 1536)
        copies.append(pltpu.make_async_copy(source.at[at], a.at[at], sems[i]))
        copies[i].start()
    for i in range(3):
        copies[i].wait()

        @pl.loop(0, 16)
        def _(g):
            place = (yh + g) % 2 * 4 + (x + g // 2) % 4
            start = place * 32 + ((core + g // 8) % 2) * 16
            at = pl.ds(pl.multiple_of(g * 48 + i * 16, 16), 16)
            for j in range(3):
                for half in range(2):
                    block = a[pl.ds(((i * 256 + start) * 3 + j) * 2 + half, 16, stride=6), :]
                    h, l = split_two(-block)
                    for term, part in enumerate((h, l, h)):
                        col = term * 768 + half * 384 + j * 128
                        out[at, col : col + 128] = part


def product_body(side, tab, matrix, *refs):
    pieces, out, held = refs[:18], refs[18], refs[19]

    def put(block, n, d):
        half = (tab[1] + n // 9) % 2
        start = pl.multiple_of(half * 384 + tab[8 + d % 8], 16)
        h, l = split_two(block)
        for i in range(3):
            for term, part in enumerate((l, h, h)):
                at = pl.ds(term * 768 + i * 128 + start, 16)
                held[at, :] = part[i * 16 : i * 16 + 16]

    @pl.loop(0, 4)
    def _(s):
        for n in range(18):
            if n % 9 < 7:
                put(pieces[n][s], n, STEPS[n % 9])
            else:

                @pl.when(s // 2 == n % 9 - 7)
                def _(n=n):
                    put(pieces[n][s % 2], n, 4)

        value = jnp.dot(
            matrix[side * 384 : side * 384 + 384, :], held[...], preferred_element_type=F32
        )
        for k in range(8):
            out[k, s] = value[k * 48 : k * 48 + 48]


def spread_body(*refs):
    rows, out, held = refs[:2], refs[2], refs[3]

    @pl.loop(0, 4)
    def _(s):
        for k in range(8):
            held[k * 48 : k * 48 + 48, :] = rows[k % 2][k // 2, s]
        h, l = split_two(held[...].T)
        for term, part in enumerate((h, l, h)):
            out[s, :, term * 384 : term * 384 + 384] = part


def pair_body(tab, keep, other, spread, *refs):
    by_x, by_y, (mine, yours, held, value) = refs[:4], refs[4:6], refs[6:]
    core = tab[2]

    @pl.loop(0, 4)
    def _(s):
        for k in range(8):
            part = keep[k, s] + other[k, s]

            @pl.when(s < 2)
            def _(k=k, part=part):
                by_x[k // 2][k % 2, s % 2] = part

            @pl.when(s >= 2)
            def _(k=k, part=part):
                by_y[k % 2][k // 2, s % 2] = part

            h, l = split_two(part)
            for term, piece in enumerate((l, h, h)):
                at = term * 384 + k * 48
                held[at : at + 48, :] = piece
        value[...] = jnp.dot(spread[s], held[...], preferred_element_type=F32)
        for out, base in ((mine, core * 128), (yours, 128 - core * 128)):
            for e in range(16):
                out[e, s] = value[pl.ds(pl.multiple_of(base + e * 8, 8), 8), :]


def first_body(a, b, c, d, e, f, *outs):
    for k in range(2):
        outs[k][...] = (a[k] + b[k]) + (c[k] + d[k])
    for k in range(4):
        outs[2 + k][...] = e[k] + f[k]


def second_body(a, b, c, d, e, f, out):
    out[0:2] = a[...] + b[...]
    out[2:4] = (c[...] + d[...]) + (e[...] + f[...])


def last_body(tab, own, other, dinv, out):
    core = tab[2]
    for k, r in enumerate((own, other)):
        base = pl.multiple_of(((core + k) % 2) * 128, 128)
        for s in range(4):
            for e in range(16):
                at = pl.ds(base + e * 8, 8)
                out[s, at, :] = dinv[s, at, :] - r[e, s]


def process(ainv, panel, diag_inv, dinv, present):
    yl, z, yh, x, core = (lax.axis_index(a) for a in AXES)
    place = jnp.arange(8, dtype=jnp.int32)
    landed = (z - place - (x * 2 + core)) % 8
    source = sum(jnp.where(landed == d, SOURCE[d], 0) for d in range(8))
    head = jnp.stack([yl * 8 + z, yl, core, x, z, yh, yh * 8 + x * 2 + core, yh]).astype(jnp.int32)
    tab = jnp.concatenate([head, (source * 16).astype(jnp.int32)])

    panel = panel.reshape(4, 48, 256)

    arrived = to_columns(panel)
    lhat, inverse = call(
        panel_body,
        [shape(4, 48, 256), shape(4, 256, 256)],
        [SMEM] + [HBM] * 3,
        [pltpu.SMEM((4, 48), jnp.int32), pltpu.VMEM((4, 48, 256), F32), DMA, DMA, DMA],
    )(tab, in_hbm(present), in_hbm(panel), in_hbm(diag_inv))
    near = [lhat] + [shift_x(lhat, -d) for d in (1, 2, 3)]
    matrix = call(
        matrix_body,
        shape(768, 2304, dtype=BF16),
        [SMEM, HBM],
        [pltpu.VMEM((4608, 128), F32), DMA, DMA, DMA],
    )(tab, in_hbm(ainv.reshape(4608, 128)))
    own = call(
        own_body,
        shape(4, 48, 256),
        [SMEM, HBM, VMEM, VMEM],
        [pltpu.SMEM((4, 48), jnp.int32), DMA],
    )(tab, in_hbm(present), arrived, inverse)
    pieces = []
    mate = swap_y(own)
    for first in (own, mate):
        ahead, back = [first], [first]
        for _ in range(3):
            ahead.append(shift_z(ahead[-1], 1))
            back.append(shift_z(back[-1], -1))
        last = [shift_z(ahead[-1][:2], 1), shift_z(back[-1][2:], -1)]
        pieces += ahead + back[1:] + last

    near = jnp.stack(near)
    far = flip_y(near)
    spread = call(
        spread_body,
        shape(4, 256, 1152, dtype=BF16),
        [VMEM] * 2,
        [pltpu.VMEM((384, 256), F32)],
    )(near, far)

    def product(side):
        return call(
            functools.partial(product_body, side),
            shape(8, 4, 48, 256),
            [SMEM] + [VMEM] * 19,
            [pltpu.VMEM((2304, 256), BF16)],
            flops=6 * 384 * 768 * 1024,
            limit=12,
        )(tab, matrix, *pieces)

    send = product(1)
    other = swap_core(send)
    keep = product(0)
    *parts, mine, yours = call(
        pair_body,
        [shape(2, 2, 48, 256)] * 4 + [shape(4, 2, 48, 256)] * 2 + [shape(16, 4, 8, 256)] * 2,
        [SMEM] + [VMEM] * 3,
        [pltpu.VMEM((1152, 256), BF16), pltpu.VMEM((256, 256), F32)],
        flops=6 * 256 * 384 * 1024,
        limit=12,
    )(tab, keep, other, spread)
    for k in (1, 2, 3):
        parts[k] = shift_x(parts[k], k)
    parts[5] = flip_y(parts[5])
    parts = list(call(first_body, [shape(2, 48, 256)] * 6, [VMEM] * 6)(*parts))
    parts[1] = flip_y(parts[1])
    for k in (1, 2, 3):
        parts[2 + k] = shift_x(parts[2 + k], k)
    shares = call(second_body, shape(4, 48, 256), [VMEM] * 6)(*parts)

    term = mine + swap_core(yours)
    total = jnp.sum(lax.all_to_all(term, PLANE, 0, 0), axis=0)
    total = lax.all_to_all(jnp.broadcast_to(total[None], (8, 4, 8, 256)), "z", 0, 0)
    total = jnp.sum(total, axis=0)
    total = lax.all_to_all(jnp.broadcast_to(total[None], (16, 4, 8, 256)), PLANE, 0, 0)
    diag = call(last_body, shape(4, 256, 256), [SMEM] + [VMEM] * 3)(
        tab, total, swap_core(total), dinv
    )
    return shares.reshape(4, 3, 1, 16, 256), diag


def solution(mesh):
    fine = Mesh(mesh.devices.reshape(2, 8, 2, 4, 2), AXES)
    rows, columns = ("y_lo", "z"), ("y_hi", "x", "core")
    return jax.shard_map(
        process,
        mesh=fine,
        in_specs=(
            P(None, rows, None, None, columns, None),
            P(None, None, rows, columns, None),
            P(),
            P(),
            P(),
        ),
        out_specs=(P(None, None, rows, columns, None), P()),
        check_vma=False,
    )
```

```python
import functools

import jax
import jax.numpy as jnp
from jax import lax
from jax.experimental import pallas as pl
from jax.experimental.pallas import tpu as pltpu
from jax.sharding import Mesh, PartitionSpec as P


F32 = jnp.float32
BF16 = jnp.bfloat16
HIGHEST = lax.Precision.HIGHEST

AXES = ("y_lo", "z", "y_hi", "x", "core")
PLANE = ("y_lo", "y_hi", "x")
LANDING = (0, 4, 1, 6, 2, 7, 3, 5)
SOURCE = tuple(LANDING.index(d) for d in range(8))
STEPS = (0, 1, 2, 3, -1, -2, -3)
SMEM = pl.BlockSpec(memory_space=pltpu.SMEM)
VMEM = pl.BlockSpec(memory_space=pltpu.VMEM)
HBM = pl.BlockSpec(memory_space=pltpu.MemorySpace.HBM)
DMA = pltpu.SemaphoreType.DMA


def to_columns(v):
    pairs = []
    for p in range(16):
        for q in range(16):
            row = (q // 8) * 8 + (p % 8 + LANDING[q % 8]) % 8
            pairs.append((p * 16 + q, row * 16 + p))
    return lax.ppermute(v, AXES, pairs)


def swap_y(v):
    return lax.ppermute(v, "y_lo", [(0, 1), (1, 0)])


def shift_z(v, d):
    return lax.ppermute(v, "z", [(p, (p + d) % 8) for p in range(8)])


def swap_core(v):
    return lax.ppermute(v, "core", [(0, 1), (1, 0)])


def flip_y(v):
    return lax.ppermute(v, "y_hi", [(0, 1), (1, 0)])


def shift_x(v, d):
    return lax.ppermute(v, "x", [(p, (p + d) % 4) for p in range(4)])


def call(body, outs, specs, scratch=(), flops=0, limit=8, aliases=None):
    return pl.pallas_call(
        body,
        out_shape=outs,
        in_specs=specs,
        out_specs=jax.tree.map(lambda _: VMEM, outs),
        scratch_shapes=list(scratch),
        input_output_aliases=aliases or {},
        compiler_params=pltpu.CompilerParams(vmem_limit_bytes=limit << 20),
        cost_estimate=pl.CostEstimate(flops=flops, transcendentals=0, bytes_accessed=4 << 20),
    )


def in_hbm(v):
    return pltpu.with_memory_space_constraint(v, pltpu.MemorySpace.HBM)


def shape(*dims, dtype=F32):
    return jax.ShapeDtypeStruct(dims, dtype)


def split_two(v):
    high = v.astype(BF16)
    return high, (v - high.astype(F32)).astype(BF16)


def panel_body(tab, present, panel, inverse, out, fetched, live, rows, *sems):
    copies = [
        pltpu.make_async_copy(*c)
        for c in zip((present, panel, inverse), (live, rows, fetched), sems)
    ]
    for c in copies:
        c.start()
    copies[1].wait()
    copies[2].wait()
    multiply(rows, fetched, out)
    copies[0].wait()
    clear(tab[0], live, out)


def own_body(tab, present, rows, inverse, out, live, sem):
    copy = pltpu.make_async_copy(present, live, sem)
    copy.start()
    multiply(rows, inverse, out)
    copy.wait()
    clear(tab[6], live, out)


def multiply(rows, inverse, out):
    for s in range(4):
        out[s] = jnp.dot(rows[s], inverse[s], precision=HIGHEST, preferred_element_type=F32)


def clear(p, live, out):
    for s in range(4):
        for i in range(3):
            at = slice(i * 16, i * 16 + 16)
            out[s, at] = out[s, at] * live[s, i * 16 + p].astype(F32)


def matrix_body(tab, source, out, rest, a, *sems):
    core, x, yh = tab[2], tab[3], tab[5]
    copies = []
    for i in range(3):
        at = pl.ds(i * 1536, 1536)
        copies.append(pltpu.make_async_copy(source.at[at], a.at[at], sems[i]))
        copies[i].start()
    for i in range(3):
        copies[i].wait()

        @pl.loop(0, 16)
        def _(g):
            place = (yh + g) % 2 * 4 + (x + g // 2) % 4
            start = place * 32 + ((core + g // 8) % 2) * 16
            at = pl.ds(pl.multiple_of(g * 48 + i * 16, 16), 16)
            for j in range(3):
                for half in range(2):
                    block = a[pl.ds(((i * 256 + start) * 3 + j) * 2 + half, 16, stride=6), :]
                    h, l = split_two(-block)
                    for term, part in enumerate((h, l, h)):
                        col = term * 768 + half * 384 + j * 128
                        out[at, col : col + 128] = part
                    h, l = split_two(-pltpu.roll(block, (128 - tab[12]) % 128, 1)[:, :16])
                    for term, part in enumerate((h, l, h)):
                        col = term * 128 + half * 48 + j * 16
                        rest[at, col : col + 16] = part
            for term in range(3):
                col = term * 128 + 96
                rest[at, col : col + 32] = jnp.zeros((16, 32), BF16)


def put(tab, out, s, block, flip, d):
    start = pl.multiple_of((tab[1] + flip) % 2 * 384 + tab[8 + d % 8], 16)
    h, l = split_two(block)
    for i in range(3):
        for term, part in enumerate((l, h, h)):
            out[s, pl.ds(term * 768 + i * 128 + start, 16), :] = part[i * 16 : i * 16 + 16]


def join_body(tab, *refs):
    out = refs[14]

    zeros = jnp.zeros((16, 256), BF16)
    base = pl.multiple_of(tab[12], 16)

    @pl.loop(0, 4)
    def _(s):
        for n in range(14):
            put(tab, out, s, refs[n][s], n // 7, STEPS[n % 7])
        for k in range(18):
            out[s, pl.ds(k * 128 + base, 16), :] = zeros


def multiply_side(side, s, matrix, joined, out):
    value = jnp.dot(
        matrix[side * 384 : side * 384 + 384, :], joined[s], preferred_element_type=F32
    )
    for k in range(8):
        out[k, s] = value[k * 48 : k * 48 + 48]


def side_body(side, matrix, joined, out):
    @pl.loop(0, 4)
    def _(s):
        multiply_side(side, s, matrix, joined, out)


def rest_body(side, tab, rest, before, a, b, c, d, out, held):
    held[...] = jnp.zeros_like(held)
    for s in range(4):
        for flip, block in enumerate(((a if s < 2 else b)[s % 2], (c if s < 2 else d)[s % 2])):
            start = pl.multiple_of((tab[1] + flip) % 2 * 48, 16)
            h, l = split_two(block)
            for i in range(3):
                for term, part in enumerate((l, h, h)):
                    at = pl.ds(term * 128 + i * 16 + start, 16)
                    held[s, at, :] = part[i * 16 : i * 16 + 16]

    @pl.loop(0, 4)
    def _(s):
        value = jnp.dot(
            rest[side * 384 : side * 384 + 384, :], held[s], preferred_element_type=F32
        )
        for k in range(8):
            out[k, s] = before[k, s] + value[k * 48 : k * 48 + 48]


def spread_body(*refs):
    rows, out, held = refs[:2], refs[2], refs[3]

    @pl.loop(0, 4)
    def _(s):
        for k in range(8):
            held[k * 48 : k * 48 + 48, :] = rows[k % 2][k // 2, s]
        h, l = split_two(held[...].T)
        for term, part in enumerate((h, l, h)):
            out[s, :, term * 384 : term * 384 + 384] = part


def pair_body(tab, keep, other, spread, mine, yours, held, value):
    core = tab[2]

    @pl.loop(0, 4)
    def _(s):
        for k in range(8):
            h, l = split_two(keep[k, s] + other[k, s])
            for term, piece in enumerate((l, h, h)):
                at = term * 384 + k * 48
                held[at : at + 48, :] = piece
        value[...] = jnp.dot(spread[s], held[...], preferred_element_type=F32)
        for out, base in ((mine, core * 128), (yours, 128 - core * 128)):
            for e in range(16):
                out[e, s] = value[pl.ds(pl.multiple_of(base + e * 8, 8), 8), :]


def parts_body(keep, other, *outs):
    by_x, by_y = outs[:4], outs[4:]
    for s in range(2):
        for k in range(8):
            by_x[k // 2][k % 2, s] = keep[k, s] + other[k, s]
            by_y[k % 2][k // 2, s] = keep[k, s + 2] + other[k, s + 2]


def level_body(pieces, out):
    total = pieces[0]
    for k in range(1, pieces.shape[0]):
        total = total + pieces[k]
    for k in range(out.shape[0]):
        out[k] = total


def first_body(a, b, c, d, e, f, *outs):
    for k in range(2):
        outs[k][...] = (a[k] + b[k]) + (c[k] + d[k])
    for k in range(4):
        outs[2 + k][...] = e[k] + f[k]


def second_body(a, b, c, d, e, f, out):
    out[0:2] = a[...] + b[...]
    out[2:4] = (c[...] + d[...]) + (e[...] + f[...])


def last_body(tab, own, other, dinv, out):
    core = tab[2]
    for k, r in enumerate((own, other)):
        base = pl.multiple_of(((core + k) % 2) * 128, 128)
        for s in range(4):
            for e in range(16):
                at = pl.ds(base + e * 8, 8)
                out[s, at, :] = dinv[s, at, :] - r[e, s]


def process(ainv, panel, diag_inv, dinv, present):
    yl, z, yh, x, core = (lax.axis_index(a) for a in AXES)
    place = jnp.arange(8, dtype=jnp.int32)
    landed = (z - place - (x * 2 + core)) % 8
    source = sum(jnp.where(landed == d, SOURCE[d], 0) for d in range(8))
    head = jnp.stack([yl * 8 + z, yl, core, x, z, yh, yh * 8 + x * 2 + core, yh]).astype(jnp.int32)
    tab = jnp.concatenate([head, (source * 16).astype(jnp.int32)])

    panel = panel.reshape(4, 48, 256)

    arrived = to_columns(panel)
    lhat, inverse = call(
        panel_body,
        [shape(4, 48, 256), shape(4, 256, 256)],
        [SMEM] + [HBM] * 3,
        [pltpu.SMEM((4, 48), jnp.int32), pltpu.VMEM((4, 48, 256), F32), DMA, DMA, DMA],
    )(tab, in_hbm(present), in_hbm(panel), in_hbm(diag_inv))
    near = [lhat] + [shift_x(lhat, -d) for d in (1, 2, 3)]
    matrix, rest = call(
        matrix_body,
        [shape(768, 2304, dtype=BF16), shape(768, 384, dtype=BF16)],
        [SMEM, HBM],
        [pltpu.VMEM((4608, 128), F32), DMA, DMA, DMA],
    )(tab, in_hbm(ainv.reshape(4608, 128)))
    own = call(
        own_body,
        shape(4, 48, 256),
        [SMEM, HBM, VMEM, VMEM],
        [pltpu.SMEM((4, 48), jnp.int32), DMA],
    )(tab, in_hbm(present), arrived, inverse)
    pieces = []
    mate = swap_y(own)
    for first in (own, mate):
        ahead, back = [first], [first]
        for _ in range(3):
            ahead.append(shift_z(ahead[-1], 1))
            back.append(shift_z(back[-1], -1))
        last = [shift_z(ahead[-1][:2], 1), shift_z(back[-1][2:], -1)]
        pieces += ahead + back[1:] + last

    near = jnp.stack(near)
    far = flip_y(near)
    spread = call(
        spread_body,
        shape(4, 256, 1152, dtype=BF16),
        [VMEM] * 2,
        [pltpu.VMEM((384, 256), F32)],
    )(near, far)

    joined = call(
        join_body, shape(4, 2304, 256, dtype=BF16), [SMEM] + [VMEM] * 14, limit=12
    )(tab, *pieces[:7], *pieces[9:16])
    halves = []
    for side in (1, 0):
        half = call(
            functools.partial(side_body, side),
            shape(8, 4, 48, 256),
            [VMEM] * 2,
            flops=6 * 384 * 768 * 1024,
            limit=16,
        )(matrix, joined)
        if side == 0:
            other = swap_core(halves[0])
        halves.append(
            call(
                functools.partial(rest_body, side),
                shape(8, 4, 48, 256),
                [SMEM] + [VMEM] * 6,
                [pltpu.VMEM((4, 384, 256), BF16)],
                flops=6 * 384 * 96 * 1024,
                limit=12,
            )(tab, rest, half, *pieces[7:9], *pieces[16:18])
        )
    keep = halves[1]
    mine, yours = call(
        pair_body,
        [shape(16, 4, 8, 256)] * 2,
        [SMEM] + [VMEM] * 3,
        [pltpu.VMEM((1152, 256), BF16), pltpu.VMEM((256, 256), F32)],
        flops=6 * 256 * 384 * 1024,
        limit=12,
    )(tab, keep, other, spread)
    parts = call(
        parts_body,
        [shape(2, 2, 48, 256)] * 4 + [shape(4, 2, 48, 256)] * 2,
        [VMEM] * 2,
    )(keep, other)
    parts = list(parts)
    for k in (1, 2, 3):
        parts[k] = shift_x(parts[k], k)
    parts[5] = flip_y(parts[5])
    parts = list(call(first_body, [shape(2, 48, 256)] * 6, [VMEM] * 6)(*parts))
    parts[1] = flip_y(parts[1])
    for k in (1, 2, 3):
        parts[2 + k] = shift_x(parts[2 + k], k)
    shares = call(second_body, shape(4, 48, 256), [VMEM] * 6)(*parts)

    yours = swap_core(yours)
    term = mine + yours
    total = lax.all_to_all(term, PLANE, 0, 0)
    total = call(level_body, shape(8, 4, 8, 256), [VMEM])(total)
    total = lax.all_to_all(total, "z", 0, 0)
    total = call(level_body, shape(16, 4, 8, 256), [VMEM])(total)
    total = lax.all_to_all(total, PLANE, 0, 0)
    diag = call(last_body, shape(4, 256, 256), [SMEM] + [VMEM] * 3)(
        tab, total, swap_core(total), dinv
    )
    return shares.reshape(4, 3, 1, 16, 256), diag


def solution(mesh):
    fine = Mesh(mesh.devices.reshape(2, 8, 2, 4, 2), AXES)
    rows, columns = ("y_lo", "z"), ("y_hi", "x", "core")
    return jax.shard_map(
        process,
        mesh=fine,
        in_specs=(
            P(None, rows, None, None, columns, None),
            P(None, None, rows, columns, None),
            P(),
            P(),
            P(),
        ),
        out_specs=(P(None, None, rows, columns, None), P()),
        check_vma=False,
    )
```

```python
import jax
import jax.numpy as jnp
from jax import lax
from jax.experimental import pallas as pl
from jax.experimental.pallas import tpu as pltpu
from jax.sharding import Mesh, PartitionSpec as P


F32 = jnp.float32
BF16 = jnp.bfloat16
HIGHEST = lax.Precision.HIGHEST

AXES = ("y_lo", "z", "y_hi", "x", "core")
PLANE = ("y_lo", "y_hi", "x")
LANDING = (0, 4, 1, 6, 2, 7, 3, 5)
SOURCE = tuple(LANDING.index(d) for d in range(8))
STEPS = (0, 1, 2, 3, -1, -2, -3)
SMEM = pl.BlockSpec(memory_space=pltpu.SMEM)
VMEM = pl.BlockSpec(memory_space=pltpu.VMEM)
HBM = pl.BlockSpec(memory_space=pltpu.MemorySpace.HBM)
DMA = pltpu.SemaphoreType.DMA


def to_columns(v):
    pairs = []
    for p in range(16):
        for q in range(16):
            row = (q // 8) * 8 + (p % 8 + LANDING[q % 8]) % 8
            pairs.append((p * 16 + q, row * 16 + p))
    return lax.ppermute(v, AXES, pairs)


def swap_y(v):
    return lax.ppermute(v, "y_lo", [(0, 1), (1, 0)])


def shift_z(v, d):
    return lax.ppermute(v, "z", [(p, (p + d) % 8) for p in range(8)])


def swap_core(v):
    return lax.ppermute(v, "core", [(0, 1), (1, 0)])


def flip_y(v):
    return lax.ppermute(v, "y_hi", [(0, 1), (1, 0)])


def shift_x(v, d):
    return lax.ppermute(v, "x", [(p, (p + d) % 4) for p in range(4)])


def call(body, outs, specs, scratch=(), flops=0, limit=8, aliases=None):
    return pl.pallas_call(
        body,
        out_shape=outs,
        in_specs=specs,
        out_specs=jax.tree.map(lambda _: VMEM, outs),
        scratch_shapes=list(scratch),
        input_output_aliases=aliases or {},
        compiler_params=pltpu.CompilerParams(vmem_limit_bytes=limit << 20),
        cost_estimate=pl.CostEstimate(flops=flops, transcendentals=0, bytes_accessed=4 << 20),
    )


def in_hbm(v):
    return pltpu.with_memory_space_constraint(v, pltpu.MemorySpace.HBM)


def shape(*dims, dtype=F32):
    return jax.ShapeDtypeStruct(dims, dtype)


def split_two(v):
    high = v.astype(BF16)
    return high, (v - high.astype(F32)).astype(BF16)


def panel_body(tab, present, panel, inverse, out, fetched, live, rows, *sems):
    copies = [
        pltpu.make_async_copy(*c)
        for c in zip((present, panel, inverse), (live, rows, fetched), sems)
    ]
    for c in copies:
        c.start()
    copies[1].wait()
    copies[2].wait()
    multiply(rows, fetched, out)
    copies[0].wait()
    clear(tab[0], live, out)


def own_body(tab, present, rows, inverse, out, live, sem):
    copy = pltpu.make_async_copy(present, live, sem)
    copy.start()
    multiply(rows, inverse, out)
    copy.wait()
    clear(tab[6], live, out)


def multiply(rows, inverse, out):
    for s in range(4):
        out[s] = jnp.dot(rows[s], inverse[s], precision=HIGHEST, preferred_element_type=F32)


def clear(p, live, out):
    for s in range(4):
        for i in range(3):
            at = slice(i * 16, i * 16 + 16)
            out[s, at] = out[s, at] * live[s, i * 16 + p].astype(F32)


def matrix_body(tab, source, out, a, *sems):
    core, x, yh = tab[2], tab[3], tab[5]
    copies = []
    for i in range(3):
        at = pl.ds(i * 1536, 1536)
        copies.append(pltpu.make_async_copy(source.at[at], a.at[at], sems[i]))
        copies[i].start()
    for i in range(3):
        copies[i].wait()

        @pl.loop(0, 16)
        def _(g):
            place = (yh + g) % 2 * 4 + (x + g // 2) % 4
            start = place * 32 + ((core + g // 8) % 2) * 16
            at = pl.ds(pl.multiple_of(g * 48 + i * 16, 16), 16)
            for j in range(3):
                for half in range(2):
                    block = a[pl.ds(((i * 256 + start) * 3 + j) * 2 + half, 16, stride=6), :]
                    h, l = split_two(-block)
                    for term, part in enumerate((h, l, h)):
                        col = term * 768 + half * 384 + j * 128
                        out[at, col : col + 128] = part


def put(tab, out, s, block, flip, d):
    start = pl.multiple_of((tab[1] + flip) % 2 * 384 + tab[8 + d % 8], 16)
    h, l = split_two(block)
    for i in range(3):
        for term, part in enumerate((l, h, h)):
            out[s, pl.ds(term * 768 + i * 128 + start, 16), :] = part[i * 16 : i * 16 + 16]


def join_body(tab, *refs):
    out = refs[14]

    @pl.loop(0, 4)
    def _(s):
        for n in range(14):
            put(tab, out, s, refs[n][s], n // 7, STEPS[n % 7])


def multiply_side(side, s, matrix, joined, out):
    value = jnp.dot(
        matrix[side * 384 : side * 384 + 384, :], joined[s], preferred_element_type=F32
    )
    for k in range(8):
        out[k, s] = value[k * 48 : k * 48 + 48]


def send_body(tab, matrix, before, a, b, c, d, out, joined):
    for s in range(4):
        put(tab, joined, s, (a if s < 2 else b)[s % 2], 0, 4)
        put(tab, joined, s, (c if s < 2 else d)[s % 2], 1, 4)

    @pl.loop(0, 4)
    def _(s):
        multiply_side(1, s, matrix, joined, out)


def keep_body(matrix, joined, out):
    @pl.loop(0, 4)
    def _(s):
        multiply_side(0, s, matrix, joined, out)


def spread_body(*refs):
    rows, out, held = refs[:2], refs[2], refs[3]

    @pl.loop(0, 4)
    def _(s):
        for k in range(8):
            held[k * 48 : k * 48 + 48, :] = rows[k % 2][k // 2, s]
        h, l = split_two(held[...].T)
        for term, part in enumerate((h, l, h)):
            out[s, :, term * 384 : term * 384 + 384] = part


def pair_body(tab, keep, other, spread, mine, yours, held, value):
    core = tab[2]

    @pl.loop(0, 4)
    def _(s):
        for k in range(8):
            h, l = split_two(keep[k, s] + other[k, s])
            for term, piece in enumerate((l, h, h)):
                at = term * 384 + k * 48
                held[at : at + 48, :] = piece
        value[...] = jnp.dot(spread[s], held[...], preferred_element_type=F32)
        for out, base in ((mine, core * 128), (yours, 128 - core * 128)):
            for e in range(16):
                out[e, s] = value[pl.ds(pl.multiple_of(base + e * 8, 8), 8), :]


def parts_body(keep, other, *outs):
    by_x, by_y = outs[:4], outs[4:]
    for s in range(2):
        for k in range(8):
            by_x[k // 2][k % 2, s] = keep[k, s] + other[k, s]
            by_y[k % 2][k // 2, s] = keep[k, s + 2] + other[k, s + 2]


def level_body(pieces, out):
    total = pieces[0]
    for k in range(1, pieces.shape[0]):
        total = total + pieces[k]
    for k in range(out.shape[0]):
        out[k] = total


def first_body(a, b, c, d, e, f, *outs):
    for k in range(2):
        outs[k][...] = (a[k] + b[k]) + (c[k] + d[k])
    for k in range(4):
        outs[2 + k][...] = e[k] + f[k]


def second_body(a, b, c, d, e, f, out):
    out[0:2] = a[...] + b[...]
    out[2:4] = (c[...] + d[...]) + (e[...] + f[...])


def last_body(tab, own, other, dinv, out):
    core = tab[2]
    for k, r in enumerate((own, other)):
        base = pl.multiple_of(((core + k) % 2) * 128, 128)
        for s in range(4):
            for e in range(16):
                at = pl.ds(base + e * 8, 8)
                out[s, at, :] = dinv[s, at, :] - r[e, s]


def process(ainv, panel, diag_inv, dinv, present):
    yl, z, yh, x, core = (lax.axis_index(a) for a in AXES)
    place = jnp.arange(8, dtype=jnp.int32)
    landed = (z - place - (x * 2 + core)) % 8
    source = sum(jnp.where(landed == d, SOURCE[d], 0) for d in range(8))
    head = jnp.stack([yl * 8 + z, yl, core, x, z, yh, yh * 8 + x * 2 + core, yh]).astype(jnp.int32)
    tab = jnp.concatenate([head, (source * 16).astype(jnp.int32)])

    panel = panel.reshape(4, 48, 256)

    arrived = to_columns(panel)
    lhat, inverse = call(
        panel_body,
        [shape(4, 48, 256), shape(4, 256, 256)],
        [SMEM] + [HBM] * 3,
        [pltpu.SMEM((4, 48), jnp.int32), pltpu.VMEM((4, 48, 256), F32), DMA, DMA, DMA],
    )(tab, in_hbm(present), in_hbm(panel), in_hbm(diag_inv))
    near = [lhat] + [shift_x(lhat, -d) for d in (1, 2, 3)]
    matrix = call(
        matrix_body,
        shape(768, 2304, dtype=BF16),
        [SMEM, HBM],
        [pltpu.VMEM((4608, 128), F32), DMA, DMA, DMA],
    )(tab, in_hbm(ainv.reshape(4608, 128)))
    own = call(
        own_body,
        shape(4, 48, 256),
        [SMEM, HBM, VMEM, VMEM],
        [pltpu.SMEM((4, 48), jnp.int32), DMA],
    )(tab, in_hbm(present), arrived, inverse)
    pieces = []
    mate = swap_y(own)
    for first in (own, mate):
        ahead, back = [first], [first]
        for _ in range(3):
            ahead.append(shift_z(ahead[-1], 1))
            back.append(shift_z(back[-1], -1))
        last = [shift_z(ahead[-1][:2], 1), shift_z(back[-1][2:], -1)]
        pieces += ahead + back[1:] + last

    near = jnp.stack(near)
    far = flip_y(near)
    spread = call(
        spread_body,
        shape(4, 256, 1152, dtype=BF16),
        [VMEM] * 2,
        [pltpu.VMEM((384, 256), F32)],
    )(near, far)

    joined = call(
        join_body, shape(4, 2304, 256, dtype=BF16), [SMEM] + [VMEM] * 14, limit=12
    )(tab, *pieces[:7], *pieces[9:16])
    send, joined = call(
        send_body,
        [shape(8, 4, 48, 256), shape(4, 2304, 256, dtype=BF16)],
        [SMEM] + [VMEM] * 6,
        flops=6 * 384 * 768 * 1024,
        limit=16,
        aliases={2: 1},
    )(tab, matrix, joined, *pieces[7:9], *pieces[16:18])
    other = swap_core(send)
    keep = call(
        keep_body, shape(8, 4, 48, 256), [VMEM] * 2, flops=6 * 384 * 768 * 1024, limit=16
    )(matrix, joined)
    mine, yours = call(
        pair_body,
        [shape(16, 4, 8, 256)] * 2,
        [SMEM] + [VMEM] * 3,
        [pltpu.VMEM((1152, 256), BF16), pltpu.VMEM((256, 256), F32)],
        flops=6 * 256 * 384 * 1024,
        limit=12,
    )(tab, keep, other, spread)
    parts = call(
        parts_body,
        [shape(2, 2, 48, 256)] * 4 + [shape(4, 2, 48, 256)] * 2,
        [VMEM] * 2,
    )(keep, other)
    parts = list(parts)
    for k in (1, 2, 3):
        parts[k] = shift_x(parts[k], k)
    parts[5] = flip_y(parts[5])
    parts = list(call(first_body, [shape(2, 48, 256)] * 6, [VMEM] * 6)(*parts))
    parts[1] = flip_y(parts[1])
    for k in (1, 2, 3):
        parts[2 + k] = shift_x(parts[2 + k], k)
    shares = call(second_body, shape(4, 48, 256), [VMEM] * 6)(*parts)

    yours = swap_core(yours)
    term = mine + yours
    total = lax.all_to_all(term, PLANE, 0, 0)
    total = call(level_body, shape(8, 4, 8, 256), [VMEM])(total)
    total = lax.all_to_all(total, "z", 0, 0)
    total = call(level_body, shape(16, 4, 8, 256), [VMEM])(total)
    total = lax.all_to_all(total, PLANE, 0, 0)
    diag = call(last_body, shape(4, 256, 256), [SMEM] + [VMEM] * 3)(
        tab, total, swap_core(total), dinv
    )
    return shares.reshape(4, 3, 1, 16, 256), diag


def solution(mesh):
    fine = Mesh(mesh.devices.reshape(2, 8, 2, 4, 2), AXES)
    rows, columns = ("y_lo", "z"), ("y_hi", "x", "core")
    return jax.shard_map(
        process,
        mesh=fine,
        in_specs=(
            P(None, rows, None, None, columns, None),
            P(None, None, rows, columns, None),
            P(),
            P(),
            P(),
        ),
        out_specs=(P(None, None, rows, columns, None), P()),
        check_vma=False,
    )
```
